256 devices in a mesh: seq: 32 (over x_lo, z, core), head: 8 (over y, x_hi).
Axes of the slice: x: 4 (x_hi: 2, x_lo: 2; x = x_hi * 2 + x_lo), y: 4, z: 8, core: 2. Of those that a mesh axis runs over, the one named last changes fastest.
Arguments:
- query: bfloat16 [36864, 3072], P(('seq', 'head')), may hold values from -6 to 6
- keys: bfloat16 [36864, 3072], P(('seq', 'head')), may hold values from -6 to 6
- values: bfloat16 [36864, 3072], P(('seq', 'head')), may hold values from -6 to 6
- windows: int32 [96, 5], P('seq'), may hold values from -1 to 95, as said below
Outputs:
- attended: bfloat16 [36864, 3072], P(('seq', 'head'))
The draws below stay inside these ranges and needn't reach their ends.
Inputs may be any that keep to these rules, and one draw needn't show every extreme that they name: `windows`: row t starts with t, then lists distinct tiles, then -1 in every remaining slot. Each listed tile other than t has a tile row within 1 of t's and lies either in t's tile-frame in t's tile column or the one beside it (tile column index within 1), or in t's tile column of the tile-frame before or after; so with s = t // 3 it lies in tile column s, s - 1, s + 1, s - 8 or s + 8.
All inputs are finite; a program needn't handle non-finite values.
Results may differ from the reference program's by a relative error of at most 0.0048.
Values may be sent and summed in bfloat16 or wider, within the bound.
No kernel may reach another device: no remote copies, remote signals or barrier semaphores. Data moves between devices by JAX's collectives and lax.ppermute only.
A program may use at most 128 MiB of HBM per device.

```python
import jax
import jax.numpy as jnp
from jax import lax

H = 24
HD = 128
TILE = 384
ROWS = 3
TFR = 4
W = 5
COLS = 8
TILES = 96
TOKENS = 36864
CH = 3072


def base_field(key, salt):
    field = jnp.clip(jax.random.normal(jax.random.fold_in(key, salt), (TOKENS, CH), jnp.float32), -6.0, 6.0)
    return field


def draw_query(key, part):
    field = base_field(key, 1)
    return field.astype(jnp.bfloat16)


def draw_keys(key, part):
    field = base_field(key, 2)
    return field.astype(jnp.bfloat16)


def draw_windows(key, part):
    tile_ids = jnp.arange(TILES, dtype=jnp.int32)
    per_frame = COLS * ROWS
    frame = tile_ids // per_frame
    column = tile_ids // ROWS % COLS
    row = tile_ids % ROWS
    frame_step = jnp.array([0, 0, 0, 0, 0, 0, 0, 0, -1, -1, -1, 1, 1, 1], dtype=jnp.int32)
    column_step = jnp.array([-1, -1, -1, 0, 0, 1, 1, 1, 0, 0, 0, 0, 0, 0], dtype=jnp.int32)
    row_step = jnp.array([-1, 0, 1, -1, 1, -1, 0, 1, -1, 0, 1, -1, 0, 1], dtype=jnp.int32)
    near_frame = frame[:, None] + frame_step[None, :]
    near_column = column[:, None] + column_step[None, :]
    near_row = row[:, None] + row_step[None, :]
    valid = (near_frame >= 0) & (near_frame < TFR) & (near_column >= 0) & (near_column < COLS) & (near_row >= 0) & (near_row < ROWS)
    named = (near_frame * COLS + near_column) * ROWS + near_row
    noise = jax.random.randint(jax.random.fold_in(key, 3), (TILES, 14), 0, 1 << 20)
    score = jnp.where(valid, noise * 16 + jnp.arange(14, dtype=jnp.int32)[None, :], 1 << 30)
    order = jnp.argsort(score, axis=1, stable=True)[:, :W - 1]
    picked = jnp.take_along_axis(named, order, axis=1)
    usable = jnp.take_along_axis(valid, order, axis=1)
    others = jnp.where(usable, picked, -1)
    return jnp.concatenate([tile_ids[:, None], others], axis=1).astype(jnp.int32)


def shard_levels(key, shape, cuts, low, largest):
    factor_of = 1.0
    for axis_at, parts in cuts:
        heights = jax.random.uniform(jax.random.fold_in(jax.random.fold_in(key, 6), axis_at), (parts,), jnp.float32, low / len(cuts), largest / len(cuts))
        factor_of = factor_of * jnp.repeat(jnp.exp(heights), shape[axis_at] // parts).reshape((-1,) + (1,) * (len(shape) - 1 - axis_at))
    return factor_of


def centred(rng, extent, deviation, bound, split=(), held_as=jnp.bfloat16):
    factor_of = shard_levels(rng, extent, split, -0.22, 0.18) if split else 1.0
    values = jax.random.normal(rng, extent, jnp.float32) * deviation * factor_of
    return jnp.minimum(jnp.maximum(values, -bound), bound).astype(held_as)


def setup_inputs(seed: int = 0) -> dict:
    seeds = jax.random.split(jax.random.key(seed), 5)
    return {
        "query": draw_query(jax.random.fold_in(seeds[4], 71), 0),
        "keys": draw_keys(jax.random.fold_in(seeds[4], 71), 0),
        "values": centred(seeds[2], (TOKENS, CH), 1.0, 6.0, ((0, 256),)),
        "windows": draw_windows(jax.random.fold_in(seeds[4], 71), 0),
    }


def reference(query, keys, values, windows):
    q_tiles = query.reshape(TILES, TILE, H, HD)
    k_tiles = keys.reshape(TILES, TILE, H, HD)
    v_tiles = values.reshape(TILES, TILE, H, HD)
    scale = 1.0 / (HD ** 0.5)

    def one_tile(item):
        q_tile, row = item
        live = row >= 0
        safe_row = jnp.maximum(row, 0).astype(jnp.int32)
        picked_k = jnp.take(k_tiles, safe_row, axis=0).reshape(W * TILE, H, HD).astype(jnp.float32)
        picked_v = jnp.take(v_tiles, safe_row, axis=0).reshape(W * TILE, H, HD).astype(jnp.float32)
        scores = jnp.einsum("qhd,khd->hqk", q_tile.astype(jnp.float32), picked_k) * scale
        key_live = jnp.repeat(live, TILE)
        scores = jnp.where(key_live[None, None, :], scores, -jnp.inf)
        top = jnp.max(scores, axis=-1, keepdims=True)
        expo = jnp.exp(scores - top)
        total = jnp.sum(expo, axis=-1)
        weights = lax.optimization_barrier(expo.astype(jnp.bfloat16)).astype(jnp.float32)
        mixed = jnp.einsum("hqk,khd->qhd", weights, picked_v)
        return (mixed / jnp.transpose(total)[:, :, None]).astype(jnp.bfloat16)

    result = lax.map(one_tile, (q_tiles, windows))
    return result.reshape(TOKENS, CH)
```

```python
import functools

import jax
import jax.numpy as jnp
from jax import lax
from jax.experimental import pallas as pl
from jax.experimental.pallas import tpu as pltpu
from jax.sharding import PartitionSpec as P

HD = 128
TFR = 4
SCALE2 = 1.4426950408889634 / HD**0.5


def attend_kernel(tile, per_slab, idx_ref, live_ref, q_ref, *rest):
    sources, (o_ref, kv, sems) = rest[:5], rest[5:]
    blocks, rows = sources[0].shape[0], sources[0].shape[2]
    copies = []
    for at, source in enumerate(sources):
        for part in range(2):
            copy = pltpu.make_async_copy(
                source.at[:, part], kv.at[part, pl.ds(at * blocks, blocks)], sems.at[at, part]
            )
            copy.start()
            copies.append(copy)
    for copy in copies:
        copy.wait()
    flat = kv.reshape(2, len(sources) * blocks * rows, HD)
    slots = idx_ref.shape[1]

    def one_tile(t, carry):
        start = pl.multiple_of(t * tile, 128)
        q = q_ref[pl.ds(start, tile), :]
        scores, tops, begins, alive = [], [], [], []
        for j in range(slots):
            begin = pl.multiple_of(idx_ref[t, j] * tile, 128)
            k = flat[0, pl.ds(begin, tile), :]
            s = lax.dot_general(q, k, (((1,), (1,)), ((), ())), preferred_element_type=jnp.float32)
            top = jnp.max(s, axis=1, keepdims=True)
            on = live_ref[t, j] > 0
            tops.append(jnp.where(on, top, -jnp.inf))
            scores.append(s)
            begins.append(begin)
            alive.append(on)
        top = functools.reduce(jnp.maximum, tops) * SCALE2
        total = jnp.zeros((tile, 1), jnp.float32)
        mixed = jnp.zeros((tile, HD), jnp.float32)
        for j in range(slots):
            shift = jnp.where(alive[j], top, jnp.inf)
            expo = jnp.exp2(scores[j] * SCALE2 - shift)
            total = total + jnp.sum(expo, axis=1, keepdims=True)
            v = flat[1, pl.ds(begins[j], tile), :]
            mixed = mixed + jnp.dot(expo.astype(jnp.bfloat16), v, preferred_element_type=jnp.float32)
        o_ref[pl.ds(start, tile), :] = (mixed / total).astype(o_ref.dtype)
        return carry

    lax.fori_loop(0, per_slab, one_tile, 0)


def attend(idx, live, q, sources):
    per_slab = idx.shape[0]
    slab = q.shape[0]
    tile = slab // per_slab
    blocks, _, rows, _ = sources[0].shape
    count = len(sources)
    keys = idx.shape[1] * tile
    return pl.pallas_call(
        functools.partial(attend_kernel, tile, per_slab),
        out_shape=jax.ShapeDtypeStruct((slab, HD), q.dtype),
        grid_spec=pltpu.PrefetchScalarGridSpec(
            num_scalar_prefetch=2,
            grid=(1,),
            in_specs=[pl.BlockSpec((slab, HD), lambda i, *_: (0, 0))]
            + [pl.BlockSpec(memory_space=pl.ANY)] * count,
            out_specs=pl.BlockSpec((slab, HD), lambda i, *_: (0, 0)),
            scratch_shapes=[
                pltpu.VMEM((2, count * blocks, rows, HD), q.dtype),
                pltpu.SemaphoreType.DMA((count, 2)),
            ],
        ),
        cost_estimate=pl.CostEstimate(
            flops=4 * slab * keys * HD, bytes_accessed=4 * slab * HD * (count + 1), transcendentals=slab * keys
        ),
        name="attend",
    )(idx, live, q, *sources)


def body(query, keys, values, windows):
    groups = lax.axis_size("head")
    peers = lax.axis_size("seq")
    columns = peers // TFR
    rows = query.shape[0]
    local = query.shape[1] // (groups * HD)
    per_slab = windows.shape[0]

    across = [(s, s ^ columns) for s in range(peers)]
    right = [(s, s + 1) for s in range(peers) if (s + 1) % columns]
    left = [(s, s - 1) for s in range(peers) if s % columns]
    middle = [(s, s + 2 * columns) for s in range(columns)] + [
        (s, s - 2 * columns) for s in range(3 * columns, peers)
    ]

    here = lax.axis_index("seq")
    live = windows >= 0
    delta = windows // per_slab - here
    partner = jnp.where(here // columns % 2 == 0, columns, -columns)
    code = jnp.where(
        delta == 0,
        0,
        jnp.where(delta == -1, 1, jnp.where(delta == 1, 2, jnp.where(delta == partner, 3, 4))),
    )
    idx = jnp.where(live, code * per_slab + windows % per_slab, 0)
    live = live.astype(jnp.int32)

    def by_group(x):
        return jnp.transpose(x.reshape(rows, groups, local, HD), (2, 1, 0, 3))

    q_parts, k_parts, v_parts = by_group(query), by_group(keys), by_group(values)

    def exchange(x):
        return lax.all_to_all(x, "head", split_axis=0, concat_axis=0, tiled=True)

    outs = []
    for i in range(local):
        own = exchange(jnp.stack([k_parts[i], v_parts[i]], axis=1))
        far = lax.ppermute(own, "seq", across)
        before = lax.ppermute(own, "seq", right)
        after = lax.ppermute(own, "seq", left)
        second = lax.ppermute(far, "seq", middle)
        q = exchange(q_parts[i]).reshape(groups * rows, HD)
        o = attend(idx, live, q, [own, before, after, far, second])
        outs.append(exchange(o.reshape(groups, rows, HD)))
    out = jnp.stack(outs, axis=1)
    return jnp.transpose(out, (2, 0, 1, 3)).reshape(rows, groups * local * HD)


def solution(mesh):
    return jax.shard_map(
        body,
        mesh=mesh,
        in_specs=(
            P(("seq", "head"), None),
            P(("seq", "head"), None),
            P(("seq", "head"), None),
            P("seq", None),
        ),
        out_specs=P(("seq", "head"), None),
        check_vma=False,
    )
```

```python
import functools

import jax
import jax.numpy as jnp
from jax import lax
from jax.experimental import pallas as pl
from jax.experimental.pallas import tpu as pltpu
from jax.sharding import PartitionSpec as P


HD = 128
TFR = 4
SCALE2 = 1.4426950408889634 / HD**0.5


ANY = pl.BlockSpec(memory_space=pl.ANY)


def after(value, *first):
    return lax.optimization_barrier((value,) + first)[0]


def pack_kernel(picks, local, count, *refs):
    arrays, o_ref, sems = refs[:count], refs[count], refs[count + 1]
    copies = []
    for at, (array, head) in enumerate(picks):
        for g in range(o_ref.shape[0]):
            copy = pltpu.make_async_copy(
                arrays[array].at[:, pl.ds((g * local + head) * HD, HD)], o_ref.at[g, at], sems.at[at, g]
            )
            copy.start()
            copies.append(copy)
    for copy in copies:
        copy.wait()


def pack(arrays, picks, groups):
    rows, width = arrays[0].shape
    shape = (groups, len(picks), rows, HD)
    return pl.pallas_call(
        functools.partial(pack_kernel, picks, width // (groups * HD), len(arrays)),
        out_shape=jax.ShapeDtypeStruct(shape, arrays[0].dtype),
        grid=(1,),
        in_specs=[ANY] * len(arrays),
        out_specs=pl.BlockSpec(shape, lambda i: (0, 0, 0, 0)),
        scratch_shapes=[pltpu.SemaphoreType.DMA((len(picks), groups))],
        cost_estimate=pl.CostEstimate(
            flops=0, bytes_accessed=4 * groups * len(picks) * rows * HD, transcendentals=0
        ),
        name="pack",
    )(*arrays)


def unpack_kernel(local, *refs):
    parts, o_ref, sems = refs[:local], refs[local], refs[local + 1]
    copies = []
    for head, part in enumerate(parts):
        for g in range(part.shape[0]):
            copy = pltpu.make_async_copy(
                part.at[g], o_ref.at[:, pl.ds((g * local + head) * HD, HD)], sems.at[head, g]
            )
            copy.start()
            copies.append(copy)
    for copy in copies:
        copy.wait()


def unpack(parts):
    local = len(parts)
    groups, rows, _ = parts[0].shape
    return pl.pallas_call(
        functools.partial(unpack_kernel, local),
        out_shape=jax.ShapeDtypeStruct((rows, groups * local * HD), parts[0].dtype),
        grid=(1,),
        in_specs=[pl.BlockSpec((groups, rows, HD), lambda i: (0, 0, 0))] * local,
        out_specs=ANY,
        scratch_shapes=[pltpu.SemaphoreType.DMA((local, groups))],
        cost_estimate=pl.CostEstimate(
            flops=0, bytes_accessed=4 * groups * local * rows * HD, transcendentals=0
        ),
        name="unpack",
    )(*parts)


def attend_kernel(tile, per_slab, places, idx_ref, live_ref, *refs):
    count = len(places)
    sources, o_ref, held, q_held, sems = refs[:count], refs[count], refs[count + 1], refs[count + 2], refs[count + 3]
    blocks, rows = sources[0].shape[0], sources[0].shape[2]
    copies = []
    for at, (source, parts) in enumerate(zip(sources, places)):
        for n, part in enumerate(parts):
            into = q_held if at == 0 else held.at[n, pl.ds((at - 1) * blocks, blocks)]
            copy = pltpu.make_async_copy(source.at[:, part], into, sems.at[at, n])
            copy.start()
            copies.append(copy)
    for copy in copies:
        copy.wait()
    flat = held.reshape(2, (count - 1) * blocks * rows, HD)
    q_flat = q_held.reshape(blocks * rows, HD)
    o_flat = o_ref.reshape(blocks * rows, HD)
    slots = idx_ref.shape[1]

    def one_tile(t, carry):
        start = pl.multiple_of(t * tile, 128)
        q = q_flat[pl.ds(start, tile), :]
        scores, tops, begins, alive = [], [], [], []
        for j in range(slots):
            begin = pl.multiple_of(idx_ref[t, j] * tile, 128)
            k = flat[0, pl.ds(begin, tile), :]
            s = lax.dot_general(q, k, (((1,), (1,)), ((), ())), preferred_element_type=jnp.float32)
            top = jnp.max(s, axis=1, keepdims=True)
            on = live_ref[t, j] > 0
            tops.append(jnp.where(on, top, -jnp.inf))
            scores.append(s)
            begins.append(begin)
            alive.append(on)
        top = functools.reduce(jnp.maximum, tops) * SCALE2
        total = jnp.zeros((tile, 1), jnp.float32)
        mixed = jnp.zeros((tile, HD), jnp.float32)
        for j in range(slots):
            shift = jnp.where(alive[j], top, jnp.inf)
            expo = jnp.exp2(scores[j] * SCALE2 - shift)
            total = total + jnp.sum(expo, axis=1, keepdims=True)
            v = flat[1, pl.ds(begins[j], tile), :]
            mixed = mixed + jnp.dot(expo.astype(jnp.bfloat16), v, preferred_element_type=jnp.float32)
        o_flat[pl.ds(start, tile), :] = (mixed / total).astype(o_ref.dtype)
        return carry

    lax.fori_loop(0, per_slab, one_tile, 0)


def attend(idx, live, sources, places):
    per_slab = idx.shape[0]
    blocks, _, rows, _ = sources[0].shape
    slab = blocks * rows
    keys = idx.shape[1] * slab // per_slab
    count = len(sources)
    dtype = sources[0].dtype
    return pl.pallas_call(
        functools.partial(attend_kernel, slab // per_slab, per_slab, places),
        out_shape=jax.ShapeDtypeStruct((blocks, rows, HD), dtype),
        grid_spec=pltpu.PrefetchScalarGridSpec(
            num_scalar_prefetch=2,
            grid=(1,),
            in_specs=[ANY] * count,
            out_specs=pl.BlockSpec((blocks, rows, HD), lambda i, *_: (0, 0, 0)),
            scratch_shapes=[
                pltpu.VMEM((2, (count - 1) * blocks, rows, HD), dtype),
                pltpu.VMEM((blocks, rows, HD), dtype),
                pltpu.SemaphoreType.DMA((count, 2)),
            ],
        ),
        cost_estimate=pl.CostEstimate(
            flops=4 * slab * keys * HD, bytes_accessed=4 * slab * HD * (count + 1), transcendentals=slab * keys
        ),
        name="attend",
    )(idx, live, *sources)


def body(query, keys, values, windows):
    groups = lax.axis_size("head")
    peers = lax.axis_size("seq")
    columns = peers // TFR
    local = query.shape[1] // (groups * HD)
    per_slab = windows.shape[0]

    across = [(s, s ^ columns) for s in range(peers)]
    right = [(s, s + 1) for s in range(peers) if (s + 1) % columns]
    left = [(s, s - 1) for s in range(peers) if s % columns]
    middle = [(s, s + 2 * columns) for s in range(columns)] + [
        (s, s - 2 * columns) for s in range(3 * columns, peers)
    ]

    def send(x, pairs):
        return lax.ppermute(x, "seq", pairs)

    def exchange(x):
        return lax.all_to_all(x, "head", split_axis=0, concat_axis=0, tiled=True)

    here = lax.axis_index("seq")
    live = windows >= 0
    delta = windows // per_slab - here
    partner = jnp.where(here // columns % 2 == 0, columns, -columns)
    code = jnp.where(
        delta == 0,
        0,
        jnp.where(delta == -1, 1, jnp.where(delta == 1, 2, jnp.where(delta == partner, 3, 4))),
    )
    idx = jnp.where(live, code * per_slab + windows % per_slab, 0)
    live = live.astype(jnp.int32)

    first = pack([keys, values], [(0, 0), (1, 0)], groups)
    crossed = send(first, across)
    rest = pack([keys, values], [(n, i) for i in range(local) for n in range(2)], groups)
    own = exchange(rest)
    q_all = pack([query], [(0, i) for i in range(local)], groups)
    own_of = [own[:, 2 * i : 2 * i + 2] for i in range(local)]
    far, second, before, behind, outs = [[None] * local for _ in range(5)]
    far[1] = send(after(own_of[1], crossed), across)
    far[0] = exchange(crossed)
    far[2] = send(after(own_of[2], far[1]), across)
    q_all = exchange(q_all)
    for i in range(local):
        before[i] = send(own_of[i], right)
        behind[i] = send(own_of[i], left)
        second[i] = send(far[i], middle)
        o = attend(
            idx,
            live,
            [q_all, own, before[i], behind[i], far[i], second[i]],
            [(i,), (2 * i, 2 * i + 1)] + [(0, 1)] * 4,
        )
        outs[i] = exchange(o)
    return unpack(outs)


def solution(mesh):
    return jax.shard_map(
        body,
        mesh=mesh,
        in_specs=(
            P(("seq", "head"), None),
            P(("seq", "head"), None),
            P(("seq", "head"), None),
            P("seq", None),
        ),
        out_specs=P(("seq", "head"), None),
        check_vma=False,
    )
```

```python
import functools

import jax
import jax.numpy as jnp
from jax import lax
from jax.experimental import pallas as pl
from jax.experimental.pallas import tpu as pltpu
from jax.sharding import PartitionSpec as P


HD = 128
TFR = 4
SCALE2 = 1.4426950408889634 / HD**0.5


ANY = pl.BlockSpec(memory_space=pl.ANY)


def after(value, *first):
    return lax.optimization_barrier((value,) + first)[0]


def pack_kernel(picks, local, count, *refs):
    arrays, o_ref, sems = refs[:count], refs[count], refs[count + 1]
    copies = []
    for at, (array, head) in enumerate(picks):
        for g in range(o_ref.shape[0]):
            source = arrays[array]
            piece = source.at[:, pl.ds((g * local + head) * HD, HD)] if len(source.shape) == 2 else source.at[g, head]
            copy = pltpu.make_async_copy(piece, o_ref.at[g, at], sems.at[at, g])
            copy.start()
            copies.append(copy)
    for copy in copies:
        copy.wait()


def pack(arrays, picks, groups):
    rows, width = arrays[0].shape
    shape = (groups, len(picks), rows, HD)
    return pl.pallas_call(
        functools.partial(pack_kernel, picks, width // (groups * HD), len(arrays)),
        out_shape=jax.ShapeDtypeStruct(shape, arrays[0].dtype),
        grid=(1,),
        in_specs=[ANY] * len(arrays),
        out_specs=pl.BlockSpec(shape, lambda i: (0, 0, 0, 0)),
        scratch_shapes=[pltpu.SemaphoreType.DMA((len(picks), groups))],
        cost_estimate=pl.CostEstimate(
            flops=0, bytes_accessed=4 * groups * len(picks) * rows * HD, transcendentals=0
        ),
        name="pack",
    )(*arrays)


def unpack_kernel(local, *refs):
    parts, o_ref, sems = refs[:local], refs[local], refs[local + 1]
    copies = []
    for head, part in enumerate(parts):
        for g in range(part.shape[0]):
            copy = pltpu.make_async_copy(
                part.at[g], o_ref.at[:, pl.ds((g * local + head) * HD, HD)], sems.at[head, g]
            )
            copy.start()
            copies.append(copy)
    for copy in copies:
        copy.wait()


def unpack(parts):
    local = len(parts)
    groups, rows, _ = parts[0].shape
    return pl.pallas_call(
        functools.partial(unpack_kernel, local),
        out_shape=jax.ShapeDtypeStruct((rows, groups * local * HD), parts[0].dtype),
        grid=(1,),
        in_specs=[pl.BlockSpec((groups, rows, HD), lambda i: (0, 0, 0))] * local,
        out_specs=ANY,
        scratch_shapes=[pltpu.SemaphoreType.DMA((local, groups))],
        cost_estimate=pl.CostEstimate(
            flops=0, bytes_accessed=4 * groups * local * rows * HD, transcendentals=0
        ),
        name="unpack",
    )(*parts)


def attend_kernel(tile, per_slab, places, idx_ref, live_ref, *refs):
    count = len(places)
    sources, o_ref, held, q_held, sems = refs[:count], refs[count], refs[count + 1], refs[count + 2], refs[count + 3]
    blocks, rows = sources[0].shape[0], sources[0].shape[2]
    copies = []
    for at, (source, parts) in enumerate(zip(sources, places)):
        for n, part in enumerate(parts):
            into = q_held if at == 0 else held.at[n, pl.ds((at - 1) * blocks, blocks)]
            copy = pltpu.make_async_copy(source.at[:, part], into, sems.at[at, n])
            copy.start()
            copies.append(copy)
    for copy in copies:
        copy.wait()
    flat = held.reshape(2, (count - 1) * blocks * rows, HD)
    q_flat = q_held.reshape(blocks * rows, HD)
    o_flat = o_ref.reshape(blocks * rows, HD)
    slots = idx_ref.shape[1]

    def one_tile(t, carry):
        start = pl.multiple_of(t * tile, 128)
        q = q_flat[pl.ds(start, tile), :]
        scores, tops, begins, alive = [], [], [], []
        for j in range(slots):
            begin = pl.multiple_of(idx_ref[t, j] * tile, 128)
            k = flat[0, pl.ds(begin, tile), :]
            s = lax.dot_general(q, k, (((1,), (1,)), ((), ())), preferred_element_type=jnp.float32)
            top = jnp.max(s, axis=1, keepdims=True)
            on = live_ref[t, j] > 0
            tops.append(jnp.where(on, top, -jnp.inf))
            scores.append(s)
            begins.append(begin)
            alive.append(on)
        top = functools.reduce(jnp.maximum, tops) * SCALE2
        total = jnp.zeros((tile, 1), jnp.float32)
        mixed = jnp.zeros((tile, HD), jnp.float32)
        for j in range(slots):
            shift = jnp.where(alive[j], top, jnp.inf)
            expo = jnp.exp2(scores[j] * SCALE2 - shift)
            total = total + jnp.sum(expo, axis=1, keepdims=True)
            v = flat[1, pl.ds(begins[j], tile), :]
            mixed = mixed + jnp.dot(expo.astype(jnp.bfloat16), v, preferred_element_type=jnp.float32)
        o_flat[pl.ds(start, tile), :] = (mixed / total).astype(o_ref.dtype)
        return carry

    lax.fori_loop(0, per_slab, one_tile, 0)


def attend(idx, live, sources, places):
    per_slab = idx.shape[0]
    blocks, _, rows, _ = sources[0].shape
    slab = blocks * rows
    keys = idx.shape[1] * slab // per_slab
    count = len(sources)
    dtype = sources[0].dtype
    return pl.pallas_call(
        functools.partial(attend_kernel, slab // per_slab, per_slab, places),
        out_shape=jax.ShapeDtypeStruct((blocks, rows, HD), dtype),
        grid_spec=pltpu.PrefetchScalarGridSpec(
            num_scalar_prefetch=2,
            grid=(1,),
            in_specs=[ANY] * count,
            out_specs=pl.BlockSpec((blocks, rows, HD), lambda i, *_: (0, 0, 0)),
            scratch_shapes=[
                pltpu.VMEM((2, (count - 1) * blocks, rows, HD), dtype),
                pltpu.VMEM((blocks, rows, HD), dtype),
                pltpu.SemaphoreType.DMA((count, 2)),
            ],
        ),
        cost_estimate=pl.CostEstimate(
            flops=4 * slab * keys * HD, bytes_accessed=4 * slab * HD * (count + 1), transcendentals=slab * keys
        ),
        name="attend",
    )(idx, live, *sources)


def body(query, keys, values, windows):
    groups = lax.axis_size("head")
    peers = lax.axis_size("seq")
    columns = peers // TFR
    local = query.shape[1] // (groups * HD)
    per_slab = windows.shape[0]

    across = [(s, s ^ columns) for s in range(peers)]
    right = [(s, s + 1) for s in range(peers) if (s + 1) % columns]
    left = [(s, s - 1) for s in range(peers) if s % columns]
    middle = [(s, s + 2 * columns) for s in range(columns)] + [
        (s, s - 2 * columns) for s in range(3 * columns, peers)
    ]

    def send(x, pairs):
        return lax.ppermute(x, "seq", pairs)

    def exchange(x):
        return lax.all_to_all(x, "head", split_axis=0, concat_axis=0, tiled=True)

    here = lax.axis_index("seq")
    live = windows >= 0
    delta = windows // per_slab - here
    partner = jnp.where(here // columns % 2 == 0, columns, -columns)
    code = jnp.where(
        delta == 0,
        0,
        jnp.where(delta == -1, 1, jnp.where(delta == 1, 2, jnp.where(delta == partner, 3, 4))),
    )
    idx = jnp.where(live, code * per_slab + windows % per_slab, 0)
    live = live.astype(jnp.int32)

    first = pack([keys, values], [(0, 0), (1, 0)], groups)
    crossed = send(first, across)
    rest = pack([keys, values], [(0, 1), (1, 1), (0, 2), (1, 2)], groups)
    rest = exchange(rest)
    most = pack(
        [keys, values, query, crossed],
        [(0, 0), (1, 0), (2, 0), (2, 1), (2, 2), (3, 0), (3, 1)],
        groups,
    )
    most = exchange(most)
    own_of = [most[:, 0:2], rest[:, 0:2], rest[:, 2:4]]
    far, second, before, behind, outs = [[None] * local for _ in range(5)]
    far[0] = most[:, 5:7]
    far[1] = send(after(own_of[1], crossed), across)
    far[2] = send(after(own_of[2], far[1]), across)
    places = [
        [(2,), (0, 1), (0, 1), (0, 1), (5, 6), (0, 1)],
        [(3,), (0, 1), (0, 1), (0, 1), (0, 1), (0, 1)],
        [(4,), (2, 3), (0, 1), (0, 1), (0, 1), (0, 1)],
    ]
    for i in (1, 0, 2):
        before[i] = send(own_of[i], right)
        behind[i] = send(own_of[i], left)
        second[i] = send(far[i], middle)
        o = attend(
            idx,
            live,
            [most, rest if i else most, before[i], behind[i], far[i] if i else most, second[i]],
            places[i],
        )
        outs[i] = exchange(o)
    return unpack(outs)


def solution(mesh):
    return jax.shard_map(
        body,
        mesh=mesh,
        in_specs=(
            P(("seq", "head"), None),
            P(("seq", "head"), None),
            P(("seq", "head"), None),
            P("seq", None),
        ),
        out_specs=P(("seq", "head"), None),
        check_vma=False,
    )
```

```python
import functools

import jax
import jax.numpy as jnp
from jax import lax
from jax.experimental import pallas as pl
from jax.experimental.pallas import tpu as pltpu
from jax.sharding import PartitionSpec as P


HD = 128
TFR = 4
PIECES = 2
SCALE2 = 1.4426950408889634 / HD**0.5


ANY = pl.BlockSpec(memory_space=pl.ANY)


def after(value, *first):
    return lax.optimization_barrier((value,) + first)[0]


def pack_kernel(picks, local, count, *refs):
    arrays, o_ref, sems = refs[:count], refs[count], refs[count + 1]
    copies = []
    for at, (array, head) in enumerate(picks):
        for g in range(o_ref.shape[0]):
            source = arrays[array]
            piece = source.at[:, pl.ds((g * local + head) * HD, HD)] if len(source.shape) == 2 else source.at[g, head]
            copy = pltpu.make_async_copy(piece, o_ref.at[g, at], sems.at[at, g])
            copy.start()
            copies.append(copy)
    for copy in copies:
        copy.wait()


def pack(arrays, picks, groups):
    rows, width = arrays[0].shape
    shape = (groups, len(picks), rows, HD)
    return pl.pallas_call(
        functools.partial(pack_kernel, picks, width // (groups * HD), len(arrays)),
        out_shape=jax.ShapeDtypeStruct(shape, arrays[0].dtype),
        grid=(1,),
        in_specs=[ANY] * len(arrays),
        out_specs=pl.BlockSpec(shape, lambda i: (0, 0, 0, 0)),
        scratch_shapes=[pltpu.SemaphoreType.DMA((len(picks), groups))],
        cost_estimate=pl.CostEstimate(
            flops=0, bytes_accessed=4 * groups * len(picks) * rows * HD, transcendentals=0
        ),
        name="pack",
    )(*arrays)


def unpack_kernel(part, o_ref, sems):
    groups, local = part.shape[:2]
    copies = []
    for head in range(local):
        for g in range(groups):
            copy = pltpu.make_async_copy(
                part.at[g, head], o_ref.at[:, pl.ds((g * local + head) * HD, HD)], sems.at[head, g]
            )
            copy.start()
            copies.append(copy)
    for copy in copies:
        copy.wait()


def unpack(part):
    groups, local, rows, _ = part.shape
    return pl.pallas_call(
        unpack_kernel,
        out_shape=jax.ShapeDtypeStruct((rows, groups * local * HD), part.dtype),
        grid=(1,),
        in_specs=[pl.BlockSpec(part.shape, lambda i: (0, 0, 0, 0))],
        out_specs=ANY,
        scratch_shapes=[pltpu.SemaphoreType.DMA((local, groups))],
        cost_estimate=pl.CostEstimate(
            flops=0, bytes_accessed=4 * groups * local * rows * HD, transcendentals=0
        ),
        name="unpack",
    )(part)


def attend_kernel(tile, per_slab, plan, count, idx_ref, live_ref, *refs):
    sources, o_ref, held, q_held, o_held, s_held, sems, o_sems = refs[:count], *refs[count:]
    heads = len(plan)
    blocks, rows = sources[0].shape[0], sources[0].shape[2]
    slab = blocks * rows
    copies = []
    for h, taken in enumerate(plan):
        for at, (source, *parts) in enumerate(taken):
            for n, part in enumerate(parts):
                into = q_held.at[h] if at == 0 else held.at[h, n, pl.ds((at - 1) * blocks, blocks)]
                copy = pltpu.make_async_copy(sources[source].at[:, part], into, sems.at[h, at, n])
                copy.start()
                copies.append((h, copy))
    flat = held.reshape(heads, 2, held.shape[2] * rows, HD)
    q_flat = q_held.reshape(heads, slab, HD)
    o_flat = o_held.reshape(heads, slab, HD)
    slots = idx_ref.shape[1]
    spans = tile // HD
    block = tile // PIECES

    def one_tile(h, t):
        start = pl.multiple_of(t * tile, 128)
        begins = [pl.multiple_of(idx_ref[t, j] * tile, 128) for j in range(slots)]
        alive = [live_ref[t, j] > 0 for j in range(slots)]
        for p in range(PIECES):
            q = q_flat[h, pl.ds(start + p * block, block), :]
            most = None
            for j in range(slots):
                k = flat[h, 0, pl.ds(begins[j], tile), :]
                s = lax.dot_general(q, k, (((1,), (1,)), ((), ())), preferred_element_type=jnp.float32)
                s_held[p, j] = s
                top = functools.reduce(jnp.maximum, [s[:, c * HD : (c + 1) * HD] for c in range(spans)])
                if j:
                    top = jnp.where(alive[j], top, -jnp.inf)
                most = top if most is None else jnp.maximum(most, top)
            top = jnp.max(most, axis=1, keepdims=True) * SCALE2
            total = mixed = None
            for j in range(slots):
                shift = jnp.where(alive[j], top, jnp.inf) if j else top
                expo = jnp.exp2(s_held[p, j] * SCALE2 - shift)
                part = functools.reduce(jnp.add, [expo[:, c * HD : (c + 1) * HD] for c in range(spans)])
                v = flat[h, 1, pl.ds(begins[j], tile), :]
                pv = jnp.dot(expo.astype(jnp.bfloat16), v, preferred_element_type=jnp.float32)
                total = part if total is None else total + part
                mixed = pv if mixed is None else mixed + pv
            total = jnp.sum(total, axis=1, keepdims=True)
            o_flat[h, pl.ds(start + p * block, block), :] = (mixed / total).astype(o_flat.dtype)

    outs = []
    for h in range(heads):
        for g, copy in copies:
            if g == h:
                copy.wait()

        def step(t, carry, h=h):
            one_tile(h, t)
            return carry

        lax.fori_loop(0, per_slab, step, 0)
        copy = pltpu.make_async_copy(o_held.at[h], o_ref.at[:, h], o_sems.at[h])
        copy.start()
        outs.append(copy)
    for copy in outs:
        copy.wait()


def attend(idx, live, sources, plan):
    per_slab, slots = idx.shape
    blocks, _, rows, _ = sources[0].shape
    slab = blocks * rows
    tile = slab // per_slab
    keys = slots * tile
    heads, columns = len(plan), len(plan[0]) - 1
    dtype = sources[0].dtype
    return pl.pallas_call(
        functools.partial(attend_kernel, tile, per_slab, plan, len(sources)),
        out_shape=jax.ShapeDtypeStruct((blocks, heads, rows, HD), dtype),
        grid_spec=pltpu.PrefetchScalarGridSpec(
            num_scalar_prefetch=2,
            grid=(1,),
            in_specs=[ANY] * len(sources),
            out_specs=ANY,
            scratch_shapes=[
                pltpu.VMEM((heads, 2, columns * blocks, rows, HD), dtype),
                pltpu.VMEM((heads, blocks, rows, HD), dtype),
                pltpu.VMEM((heads, blocks, rows, HD), dtype),
                pltpu.VMEM((PIECES, slots, tile // PIECES, tile), jnp.float32),
                pltpu.SemaphoreType.DMA((heads, columns + 1, 2)),
                pltpu.SemaphoreType.DMA((heads,)),
            ],
        ),
        cost_estimate=pl.CostEstimate(
            flops=4 * heads * slab * keys * HD,
            bytes_accessed=4 * heads * slab * HD * (columns + 1),
            transcendentals=heads * slab * keys,
        ),
        name="attend",
    )(idx, live, *sources)


def body(query, keys, values, windows):
    groups = lax.axis_size("head")
    peers = lax.axis_size("seq")
    columns = peers // TFR
    per_slab = windows.shape[0]

    across = [(s, s ^ columns) for s in range(peers)]
    right = [(s, s + 1) for s in range(peers) if (s + 1) % columns]
    left = [(s, s - 1) for s in range(peers) if s % columns]
    middle = [(s, s + 2 * columns) for s in range(columns)] + [
        (s, s - 2 * columns) for s in range(3 * columns, peers)
    ]

    def send(x, pairs):
        return lax.ppermute(x, "seq", pairs)

    def exchange(x):
        return lax.all_to_all(x, "head", split_axis=0, concat_axis=0, tiled=True)

    here = lax.axis_index("seq")
    live = windows >= 0
    delta = windows // per_slab - here
    partner = jnp.where(here // columns % 2 == 0, columns, -columns)
    code = jnp.where(
        delta == 0,
        0,
        jnp.where(delta == -1, 1, jnp.where(delta == 1, 2, jnp.where(delta == partner, 3, 4))),
    )
    idx = jnp.where(live, code * per_slab + windows % per_slab, 0)
    live = live.astype(jnp.int32)

    first = pack([keys, values], [(0, 0), (1, 0)], groups)
    crossed = send(first, across)
    rest = pack([keys, values], [(0, 1), (1, 1), (0, 2), (1, 2)], groups)
    rest = exchange(rest)
    most = pack(
        [keys, values, query, crossed],
        [(0, 0), (1, 0), (2, 0), (2, 1), (2, 2), (3, 0), (3, 1)],
        groups,
    )
    most = exchange(most)
    far1 = send(after(rest[:, 0:2], crossed), across)
    far2 = send(after(rest[:, 2:4], crossed), across)
    own0 = most[:, 0:2]
    before12 = send(rest, right)
    behind12 = send(rest, left)
    before0 = send(own0, right)
    behind0 = send(own0, left)
    second0 = send(most[:, 5:7], middle)
    second1 = send(far1, middle)
    second2 = send(far2, middle)
    sources = [most, rest, before0, behind0, before12, behind12, far1, far2, second0, second1, second2]
    plan = [
        [(0, 2), (0, 0, 1), (2, 0, 1), (3, 0, 1), (0, 5, 6), (8, 0, 1)],
        [(0, 3), (1, 0, 1), (4, 0, 1), (5, 0, 1), (6, 0, 1), (9, 0, 1)],
        [(0, 4), (1, 2, 3), (4, 2, 3), (5, 2, 3), (7, 0, 1), (10, 0, 1)],
    ]
    o = attend(idx, live, sources, plan)
    o = exchange(o)
    return unpack(o)


def solution(mesh):
    return jax.shard_map(
        body,
        mesh=mesh,
        in_specs=(
            P(("seq", "head"), None),
            P(("seq", "head"), None),
            P(("seq", "head"), None),
            P("seq", None),
        ),
        out_specs=P(("seq", "head"), None),
        check_vma=False,
    )
```

```python
import functools

import jax
import jax.numpy as jnp
from jax import lax
from jax.experimental import pallas as pl
from jax.experimental.pallas import tpu as pltpu
from jax.sharding import PartitionSpec as P


HD = 128
TFR = 4
PIECES = 1
SWAPPED = 2
SCALE2 = 1.4426950408889634 / HD**0.5


ANY = pl.BlockSpec(memory_space=pl.ANY)


def after(value, *first):
    return lax.optimization_barrier((value,) + first)[0]


def lane(g, head, local, swap):
    return pl.multiple_of(((g if swap is None else jnp.bitwise_xor(g, swap)) * local + head) * HD, HD)


def pack_kernel(picks, local, count, swap_ref, *refs):
    arrays, o_ref, sems = refs[:count], refs[count], refs[count + 1]
    copies = []
    for at, (array, head) in enumerate(picks):
        swap = swap_ref[0] if head == SWAPPED else None
        for g in range(o_ref.shape[0]):
            piece = arrays[array].at[:, pl.ds(lane(g, head, local, swap), HD)]
            copy = pltpu.make_async_copy(piece, o_ref.at[g, at], sems.at[at, g])
            copy.start()
            copies.append(copy)
    for copy in copies:
        copy.wait()


def pack(swap, arrays, picks, groups):
    rows, width = arrays[0].shape
    shape = (groups, len(picks), rows, HD)
    return pl.pallas_call(
        functools.partial(pack_kernel, picks, width // (groups * HD), len(arrays)),
        out_shape=jax.ShapeDtypeStruct(shape, arrays[0].dtype),
        grid_spec=pltpu.PrefetchScalarGridSpec(
            num_scalar_prefetch=1,
            grid=(1,),
            in_specs=[ANY] * len(arrays),
            out_specs=pl.BlockSpec(shape, lambda i, *_: (0, 0, 0, 0)),
            scratch_shapes=[pltpu.SemaphoreType.DMA((len(picks), groups))],
        ),
        cost_estimate=pl.CostEstimate(
            flops=0, bytes_accessed=4 * groups * len(picks) * rows * HD, transcendentals=0
        ),
        name="pack",
    )(swap, *arrays)


def unpack_kernel(swap_ref, part, o_ref, sems):
    groups, local = part.shape[:2]
    copies = []
    for head in range(local):
        swap = swap_ref[0] if head == SWAPPED else None
        for g in range(groups):
            copy = pltpu.make_async_copy(
                part.at[g, head], o_ref.at[:, pl.ds(lane(g, head, local, swap), HD)], sems.at[head, g]
            )
            copy.start()
            copies.append(copy)
    for copy in copies:
        copy.wait()


def unpack(swap, part):
    groups, local, rows, _ = part.shape
    return pl.pallas_call(
        unpack_kernel,
        out_shape=jax.ShapeDtypeStruct((rows, groups * local * HD), part.dtype),
        grid_spec=pltpu.PrefetchScalarGridSpec(
            num_scalar_prefetch=1,
            grid=(1,),
            in_specs=[pl.BlockSpec(part.shape, lambda i, *_: (0, 0, 0, 0))],
            out_specs=ANY,
            scratch_shapes=[pltpu.SemaphoreType.DMA((local, groups))],
        ),
        cost_estimate=pl.CostEstimate(
            flops=0, bytes_accessed=4 * groups * local * rows * HD, transcendentals=0
        ),
        name="unpack",
    )(swap, part)


def attend_kernel(tile, per_slab, plan, outs_at, count, idx_ref, live_ref, *refs):
    sources, refs = refs[:count], refs[count:]
    o_ref, held, q_held, o_held, s_held, sems, o_sems = refs[-7:]
    heads = len(plan)
    blocks, rows = sources[0].shape[0], sources[0].shape[2]
    slab = blocks * rows
    copies = []
    for h, taken in enumerate(plan):
        for at, parts in enumerate(taken):
            for n, (source, part) in enumerate(parts):
                into = q_held.at[h] if at == 0 else held.at[h, n, pl.ds((at - 1) * blocks, blocks)]
                copy = pltpu.make_async_copy(sources[source].at[:, part], into, sems.at[h, at, n])
                copy.start()
                copies.append((h, copy))
    flat = held.reshape(heads, 2, held.shape[2] * rows, HD)
    q_flat = q_held.reshape(heads, slab, HD)
    o_flat = o_held.reshape(heads, slab, HD)
    slots = idx_ref.shape[1]
    spans = tile // HD
    block = tile // PIECES

    begins = [[pl.multiple_of(idx_ref[t, j] * tile, 128) for j in range(slots)] for t in range(per_slab)]
    alive = [[live_ref[t, j] > 0 for j in range(slots)] for t in range(per_slab)]
    items = [(h, t, p) for h in range(heads) for t in range(per_slab) for p in range(PIECES)]

    def score(n, j, most):
        h, t, p = items[n]
        q = q_flat[h, pl.ds(t * tile + p * block, block), :]
        k = flat[h, 0, pl.ds(begins[t][j], tile), :]
        s = lax.dot_general(q, k, (((1,), (1,)), ((), ())), preferred_element_type=jnp.float32)
        s_held[n % 2, j] = s
        top = functools.reduce(jnp.maximum, [s[:, c * HD : (c + 1) * HD] for c in range(spans)])
        if j:
            top = jnp.where(alive[t][j], top, -jnp.inf)
        return top if most is None else jnp.maximum(most, top)

    def mix(n, j, top, total, mixed):
        h, t, _ = items[n]
        shift = jnp.where(alive[t][j], top, jnp.inf) if j else top
        expo = jnp.exp2(s_held[n % 2, j] * SCALE2 - shift)
        part = functools.reduce(jnp.add, [expo[:, c * HD : (c + 1) * HD] for c in range(spans)])
        v = flat[h, 1, pl.ds(begins[t][j], tile), :]
        pv = jnp.dot(expo.astype(jnp.bfloat16), v, preferred_element_type=jnp.float32)
        return (part, pv) if total is None else (total + part, mixed + pv)

    def arrive(head):
        for h, copy in copies:
            if h == head:
                copy.wait()

    arrive(0)
    most = None
    for j in range(slots):
        most = score(0, j, most)
    outs = []
    for n, (h, t, p) in enumerate(items):
        if n + 1 < len(items) and items[n + 1][0] != h:
            arrive(h + 1)
        top = jnp.max(most, axis=1, keepdims=True) * SCALE2
        most = total = mixed = None
        for j in range(slots):
            if n + 1 < len(items):
                most = score(n + 1, j, most)
            total, mixed = mix(n, j, top, total, mixed)
        total = jnp.sum(total, axis=1, keepdims=True)
        o_flat[h, pl.ds(t * tile + p * block, block), :] = (mixed / total).astype(o_flat.dtype)
        if t == per_slab - 1 and p == PIECES - 1:
            copy = pltpu.make_async_copy(o_held.at[h], o_ref.at[:, outs_at[h]], o_sems.at[h])
            copy.start()
            outs.append(copy)
    for copy in outs:
        copy.wait()


def attend(idx, live, sources, plan, outs_at, parts, into=None):
    per_slab, slots = idx.shape
    blocks, _, rows, _ = sources[0].shape
    slab = blocks * rows
    tile = slab // per_slab
    keys = slots * tile
    heads, columns = len(plan), len(plan[0]) - 1
    dtype = sources[0].dtype
    count = len(sources)
    held = [] if into is None else [into]
    return pl.pallas_call(
        functools.partial(attend_kernel, tile, per_slab, plan, outs_at, count),
        out_shape=jax.ShapeDtypeStruct((blocks, parts, rows, HD), dtype),
        grid_spec=pltpu.PrefetchScalarGridSpec(
            num_scalar_prefetch=2,
            grid=(1,),
            in_specs=[ANY] * (count + len(held)),
            out_specs=ANY,
            scratch_shapes=[
                pltpu.VMEM((heads, 2, columns * blocks, rows, HD), dtype),
                pltpu.VMEM((heads, blocks, rows, HD), dtype),
                pltpu.VMEM((heads, blocks, rows, HD), dtype),
                pltpu.VMEM((2, slots, tile // PIECES, tile), jnp.float32),
                pltpu.SemaphoreType.DMA((heads, columns + 1, 2)),
                pltpu.SemaphoreType.DMA((heads,)),
            ],
        ),
        input_output_aliases={2 + count: 0} if held else {},
        cost_estimate=pl.CostEstimate(
            flops=4 * heads * slab * keys * HD,
            bytes_accessed=4 * heads * slab * HD * (columns + 1),
            transcendentals=heads * slab * keys,
        ),
        name="attend",
    )(idx, live, *sources, *held)


def body(query, keys, values, windows):
    groups = lax.axis_size("head")
    peers = lax.axis_size("seq")
    columns = peers // TFR
    local = query.shape[1] // (groups * HD)
    per_slab = windows.shape[0]

    across = [(s, s ^ columns) for s in range(peers)]
    right = [(s, s + 1) for s in range(peers) if (s + 1) % columns]
    left = [(s, s - 1) for s in range(peers) if s % columns]
    middle = [(s, s + 2 * columns) for s in range(columns)] + [
        (s, s - 2 * columns) for s in range(3 * columns, peers)
    ]

    def send(x, pairs):
        return lax.ppermute(x, "seq", pairs)

    def exchange(x):
        return lax.all_to_all(x, "head", split_axis=0, concat_axis=0, tiled=True)

    here = lax.axis_index("seq")
    live = windows >= 0
    delta = windows // per_slab - here
    partner = jnp.where(here // columns % 2 == 0, columns, -columns)
    code = jnp.where(
        delta == 0,
        0,
        jnp.where(delta == -1, 1, jnp.where(delta == 1, 2, jnp.where(delta == partner, 3, 4))),
    )
    idx = jnp.where(live, code * per_slab + windows % per_slab, 0)
    live = live.astype(jnp.int32)

    swap = (here >= peers // 2).astype(jnp.int32).reshape(1)
    hop = [(s * groups + h, d * groups + (h ^ 1)) for s, d in middle for h in range(groups)]

    first = pack(swap, [keys, values], [(0, 0), (1, 0), (0, 1)], groups)
    crossed = send(first, across)
    rest = pack(swap, [keys, values], [(1, 1), (0, 2), (1, 2)], groups)
    rest = exchange(rest)
    most = pack(swap, [keys, values, query], [(2, 0), (2, 1), (2, 2), (0, 0), (1, 0), (0, 1)], groups)
    most = exchange(most)
    far = send(after(rest, crossed), across)
    crossed = exchange(crossed)
    before_a = send(rest, right)
    behind_a = send(rest, left)
    own = most[:, 3:6]
    before_b = send(own, right)
    behind_b = send(own, left)
    second_2 = lax.ppermute(far[:, 1:3], ("seq", "head"), hop)
    second_1 = send(far[:, 0:1], middle)
    second_b = send(crossed, middle)
    parts = local
    plan_2 = [[((0, 2),), ((1, 1), (1, 2)), ((2, 1), (2, 2)), ((3, 1), (3, 2)), ((4, 1), (4, 2)), ((5, 0), (5, 1))]]
    o = attend(idx, live, [most, rest, before_a, behind_a, far, second_2], plan_2, (2,), parts)
    sources = [most, rest, before_a, behind_a, far, second_1, before_b, behind_b, crossed, second_b]
    plan = [
        [((0, 0),), ((0, 3), (0, 4)), ((6, 0), (6, 1)), ((7, 0), (7, 1)), ((8, 0), (8, 1)), ((9, 0), (9, 1))],
        [((0, 1),), ((0, 5), (1, 0)), ((6, 2), (2, 0)), ((7, 2), (3, 0)), ((8, 2), (4, 0)), ((9, 2), (5, 0))],
    ]
    o = attend(idx, live, sources, plan, (0, 1), parts, o)
    o = exchange(o)
    return unpack(swap, o)


def solution(mesh):
    return jax.shard_map(
        body,
        mesh=mesh,
        in_specs=(
            P(("seq", "head"), None),
            P(("seq", "head"), None),
            P(("seq", "head"), None),
            P("seq", None),
        ),
        out_specs=P(("seq", "head"), None),
        check_vma=False,
    )
```

```python
import functools

import jax
import jax.numpy as jnp
from jax import lax
from jax.experimental import pallas as pl
from jax.experimental.pallas import tpu as pltpu
from jax.sharding import PartitionSpec as P


HD = 128
TFR = 4
PIECES = 1
SWAPPED = 2
SCALE2 = 1.4426950408889634 / HD**0.5


ANY = pl.BlockSpec(memory_space=pl.ANY)


def after(value, *first):
    return lax.optimization_barrier((value,) + first)[0]


def lane(g, head, local, swap):
    return pl.multiple_of(((g if swap is None else jnp.bitwise_xor(g, swap)) * local + head) * HD, HD)


def pack_kernel(picks, local, count, swap_ref, *refs):
    arrays, o_ref, sems = refs[:count], refs[count], refs[count + 1]
    copies = []
    for at, (array, head) in enumerate(picks):
        swap = swap_ref[0] if head == SWAPPED else None
        for g in range(o_ref.shape[0]):
            piece = arrays[array].at[:, pl.ds(lane(g, head, local, swap), HD)]
            copy = pltpu.make_async_copy(piece, o_ref.at[g, at], sems.at[at, g])
            copy.start()
            copies.append(copy)
    for copy in copies:
        copy.wait()


def pack(swap, arrays, picks, groups):
    rows, width = arrays[0].shape
    shape = (groups, len(picks), rows, HD)
    return pl.pallas_call(
        functools.partial(pack_kernel, picks, width // (groups * HD), len(arrays)),
        out_shape=jax.ShapeDtypeStruct(shape, arrays[0].dtype),
        grid_spec=pltpu.PrefetchScalarGridSpec(
            num_scalar_prefetch=1,
            grid=(1,),
            in_specs=[ANY] * len(arrays),
            out_specs=pl.BlockSpec(shape, lambda i, *_: (0, 0, 0, 0)),
            scratch_shapes=[pltpu.SemaphoreType.DMA((len(picks), groups))],
        ),
        cost_estimate=pl.CostEstimate(
            flops=0, bytes_accessed=4 * groups * len(picks) * rows * HD, transcendentals=0
        ),
        name="pack",
    )(swap, *arrays)


def unpack_kernel(swap_ref, part, o_ref, sems):
    groups, local = part.shape[:2]
    copies = []
    for head in range(local):
        swap = swap_ref[0] if head == SWAPPED else None
        for g in range(groups):
            copy = pltpu.make_async_copy(
                part.at[g, head], o_ref.at[:, pl.ds(lane(g, head, local, swap), HD)], sems.at[head, g]
            )
            copy.start()
            copies.append(copy)
    for copy in copies:
        copy.wait()


def unpack(swap, part):
    groups, local, rows, _ = part.shape
    return pl.pallas_call(
        unpack_kernel,
        out_shape=jax.ShapeDtypeStruct((rows, groups * local * HD), part.dtype),
        grid_spec=pltpu.PrefetchScalarGridSpec(
            num_scalar_prefetch=1,
            grid=(1,),
            in_specs=[pl.BlockSpec(part.shape, lambda i, *_: (0, 0, 0, 0))],
            out_specs=ANY,
            scratch_shapes=[pltpu.SemaphoreType.DMA((local, groups))],
        ),
        cost_estimate=pl.CostEstimate(
            flops=0, bytes_accessed=4 * groups * local * rows * HD, transcendentals=0
        ),
        name="unpack",
    )(swap, part)


def attend_kernel(tile, per_slab, plan, outs_at, count, idx_ref, live_ref, *refs):
    sources, refs = refs[:count], refs[count:]
    o_ref, held, q_held, o_held, s_held, sems, o_sems = refs[-7:]
    heads = len(plan)
    blocks, rows = sources[0].shape[0], sources[0].shape[2]
    slab = blocks * rows
    copies = []
    for h, taken in enumerate(plan):
        for at, parts in enumerate(taken):
            for n, (source, part) in enumerate(parts):
                into = q_held.at[h] if at == 0 else held.at[h, n, pl.ds((at - 1) * blocks, blocks)]
                copy = pltpu.make_async_copy(sources[source].at[:, part], into, sems.at[h, at, n])
                copy.start()
                copies.append((h, copy))
    flat = held.reshape(heads, 2, held.shape[2] * rows, HD)
    q_flat = q_held.reshape(heads, slab, HD)
    o_flat = o_held.reshape(heads, slab, HD)
    slots = idx_ref.shape[1]
    spans = tile // HD
    block = tile // PIECES

    begins = [[pl.multiple_of(idx_ref[t, j] * tile, 128) for j in range(slots)] for t in range(per_slab)]
    alive = [[live_ref[t, j] > 0 for j in range(slots)] for t in range(per_slab)]
    items = [(h, t, p) for h in range(heads) for t in range(per_slab) for p in range(PIECES)]

    def score(n, j, most):
        h, t, p = items[n]
        q = q_flat[h, pl.ds(t * tile + p * block, block), :]
        k = flat[h, 0, pl.ds(begins[t][j], tile), :]
        s = lax.dot_general(q, k, (((1,), (1,)), ((), ())), preferred_element_type=jnp.float32)
        s_held[n % 2, j] = s
        top = functools.reduce(jnp.maximum, [s[:, c * HD : (c + 1) * HD] for c in range(spans)])
        if j:
            top = jnp.where(alive[t][j], top, -jnp.inf)
        return top if most is None else jnp.maximum(most, top)

    def mix(n, j, top, total, mixed):
        h, t, _ = items[n]
        shift = jnp.where(alive[t][j], top, jnp.inf) if j else top
        expo = jnp.exp2(s_held[n % 2, j] * SCALE2 - shift)
        part = functools.reduce(jnp.add, [expo[:, c * HD : (c + 1) * HD] for c in range(spans)])
        v = flat[h, 1, pl.ds(begins[t][j], tile), :]
        pv = jnp.dot(expo.astype(jnp.bfloat16), v, preferred_element_type=jnp.float32)
        return (part, pv) if total is None else (total + part, mixed + pv)

    def arrive(head):
        for h, copy in copies:
            if h == head:
                copy.wait()

    arrive(0)
    most = None
    for j in range(slots):
        most = score(0, j, most)
    outs = []
    for n, (h, t, p) in enumerate(items):
        if n + 1 < len(items) and items[n + 1][0] != h:
            arrive(h + 1)
        top = jnp.max(most, axis=1, keepdims=True) * SCALE2
        most = total = mixed = None
        for j in range(slots):
            if n + 1 < len(items):
                most = score(n + 1, j, most)
            total, mixed = mix(n, j, top, total, mixed)
        total = jnp.sum(total, axis=1, keepdims=True)
        o_flat[h, pl.ds(t * tile + p * block, block), :] = (mixed / total).astype(o_flat.dtype)
        if t == per_slab - 1 and p == PIECES - 1:
            copy = pltpu.make_async_copy(o_held.at[h], o_ref.at[:, outs_at[h]], o_sems.at[h])
            copy.start()
            outs.append(copy)
    for copy in outs:
        copy.wait()


def attend(idx, live, sources, plan, outs_at, parts, into=None):
    per_slab, slots = idx.shape
    blocks, _, rows, _ = sources[0].shape
    slab = blocks * rows
    tile = slab // per_slab
    keys = slots * tile
    heads, columns = len(plan), len(plan[0]) - 1
    dtype = sources[0].dtype
    count = len(sources)
    held = [] if into is None else [into]
    return pl.pallas_call(
        functools.partial(attend_kernel, tile, per_slab, plan, outs_at, count),
        out_shape=jax.ShapeDtypeStruct((blocks, parts, rows, HD), dtype),
        grid_spec=pltpu.PrefetchScalarGridSpec(
            num_scalar_prefetch=2,
            grid=(1,),
            in_specs=[ANY] * (count + len(held)),
            out_specs=ANY,
            scratch_shapes=[
                pltpu.VMEM((heads, 2, columns * blocks, rows, HD), dtype),
                pltpu.VMEM((heads, blocks, rows, HD), dtype),
                pltpu.VMEM((heads, blocks, rows, HD), dtype),
                pltpu.VMEM((2, slots, tile // PIECES, tile), jnp.float32),
                pltpu.SemaphoreType.DMA((heads, columns + 1, 2)),
                pltpu.SemaphoreType.DMA((heads,)),
            ],
        ),
        input_output_aliases={2 + count: 0} if held else {},
        cost_estimate=pl.CostEstimate(
            flops=4 * heads * slab * keys * HD,
            bytes_accessed=4 * heads * slab * HD * (columns + 1),
            transcendentals=heads * slab * keys,
        ),
        name="attend",
    )(idx, live, *sources, *held)


def body(query, keys, values, windows):
    groups = lax.axis_size("head")
    peers = lax.axis_size("seq")
    columns = peers // TFR
    local = query.shape[1] // (groups * HD)
    per_slab = windows.shape[0]

    across = [(s, s ^ columns) for s in range(peers)]
    right = [(s, s + 1) for s in range(peers) if (s + 1) % columns]
    left = [(s, s - 1) for s in range(peers) if s % columns]
    middle = [(s, s + 2 * columns) for s in range(columns)] + [
        (s, s - 2 * columns) for s in range(3 * columns, peers)
    ]

    def send(x, pairs):
        return lax.ppermute(x, "seq", pairs)

    def exchange(x):
        return lax.all_to_all(x, "head", split_axis=0, concat_axis=0, tiled=True)

    here = lax.axis_index("seq")
    live = windows >= 0
    delta = windows // per_slab - here
    partner = jnp.where(here // columns % 2 == 0, columns, -columns)
    code = jnp.where(
        delta == 0,
        0,
        jnp.where(delta == -1, 1, jnp.where(delta == 1, 2, jnp.where(delta == partner, 3, 4))),
    )
    idx = jnp.where(live, code * per_slab + windows % per_slab, 0)
    live = live.astype(jnp.int32)

    swap = (here >= peers // 2).astype(jnp.int32).reshape(1)
    hop = [(s * groups + h, d * groups + (h ^ 1)) for s, d in middle for h in range(groups)]

    first = pack(swap, [keys, values], [(0, 0), (1, 0), (0, 1)], groups)
    crossed = send(first, across)
    rest = pack(swap, [keys, values], [(1, 1), (0, 2), (1, 2)], groups)
    rest = exchange(rest)
    most = pack(swap, [keys, values, query], [(2, 0), (2, 1), (2, 2), (0, 0), (1, 0), (0, 1)], groups)
    most = exchange(most)
    far = send(after(rest, crossed), across)
    crossed = exchange(crossed)
    before_a = send(rest, right)
    behind_a = send(rest, left)
    own = most[:, 3:6]
    before_b = send(own, right)
    behind_b = send(own, left)
    second_2 = lax.ppermute(far[:, 1:3], ("seq", "head"), hop)
    second_1 = send(far[:, 0:1], middle)
    second_b = send(crossed, middle)
    parts = local
    plan_0 = [[((0, 0),), ((0, 3), (0, 4)), ((1, 0), (1, 1)), ((2, 0), (2, 1)), ((3, 0), (3, 1)), ((4, 0), (4, 1))]]
    o = attend(idx, live, [most, before_b, behind_b, crossed, second_b], plan_0, (0,), parts)
    sources = [most, rest, before_a, behind_a, far, second_1, before_b, behind_b, crossed, second_b, second_2]
    plan = [
        [((0, 1),), ((0, 5), (1, 0)), ((6, 2), (2, 0)), ((7, 2), (3, 0)), ((8, 2), (4, 0)), ((9, 2), (5, 0))],
        [((0, 2),), ((1, 1), (1, 2)), ((2, 1), (2, 2)), ((3, 1), (3, 2)), ((4, 1), (4, 2)), ((10, 0), (10, 1))],
    ]
    o = attend(idx, live, sources, plan, (1, 2), parts, o)
    o = exchange(o)
    return unpack(swap, o)


def solution(mesh):
    return jax.shard_map(
        body,
        mesh=mesh,
        in_specs=(
            P(("seq", "head"), None),
            P(("seq", "head"), None),
            P(("seq", "head"), None),
            P("seq", None),
        ),
        out_specs=P(("seq", "head"), None),
        check_vma=False,
    )
```

```python
import functools

import jax
import jax.numpy as jnp
from jax import lax
from jax.experimental import pallas as pl
from jax.experimental.pallas import tpu as pltpu
from jax.sharding import PartitionSpec as P


HD = 128
TFR = 4
PIECES = 1
SWAPPED = 2
SCALE2 = 1.4426950408889634 / HD**0.5


ANY = pl.BlockSpec(memory_space=pl.ANY)


def lane(g, head, local, swap):
    return pl.multiple_of(((g if swap is None else jnp.bitwise_xor(g, swap)) * local + head) * HD, HD)


def pack_kernel(picks, local, count, swap_ref, *refs):
    arrays, o_ref, sems = refs[:count], refs[count], refs[count + 1]
    copies = []
    for at, (array, head) in enumerate(picks):
        swap = swap_ref[0] if head == SWAPPED else None
        for g in range(o_ref.shape[0]):
            piece = arrays[array].at[:, pl.ds(lane(g, head, local, swap), HD)]
            copy = pltpu.make_async_copy(piece, o_ref.at[g, at], sems.at[at, g])
            copy.start()
            copies.append(copy)
    for copy in copies:
        copy.wait()


def pack(swap, arrays, picks, groups):
    rows, width = arrays[0].shape
    shape = (groups, len(picks), rows, HD)
    return pl.pallas_call(
        functools.partial(pack_kernel, picks, width // (groups * HD), len(arrays)),
        out_shape=jax.ShapeDtypeStruct(shape, arrays[0].dtype),
        grid_spec=pltpu.PrefetchScalarGridSpec(
            num_scalar_prefetch=1,
            grid=(1,),
            in_specs=[ANY] * len(arrays),
            out_specs=pl.BlockSpec(shape, lambda i, *_: (0, 0, 0, 0)),
            scratch_shapes=[pltpu.SemaphoreType.DMA((len(picks), groups))],
        ),
        cost_estimate=pl.CostEstimate(
            flops=0, bytes_accessed=4 * groups * len(picks) * rows * HD, transcendentals=0
        ),
        name="pack",
    )(swap, *arrays)


def unpack_kernel(swap_ref, part, o_ref, held, in_sems, sems):
    groups, local = part.shape[:2]
    arriving, leaving = [], []
    for g in range(groups):
        copy = pltpu.make_async_copy(part.at[g], held.at[g], in_sems.at[g])
        copy.start()
        arriving.append(copy)
    for g in range(groups):
        arriving[g].wait()
        for head in range(local):
            swap = swap_ref[0] if head == SWAPPED else None
            copy = pltpu.make_async_copy(
                held.at[g, head], o_ref.at[:, pl.ds(lane(g, head, local, swap), HD)], sems.at[head, g]
            )
            copy.start()
            leaving.append(copy)
    for copy in leaving:
        copy.wait()


def unpack(swap, part):
    groups, local, rows, _ = part.shape
    return pl.pallas_call(
        unpack_kernel,
        out_shape=jax.ShapeDtypeStruct((rows, groups * local * HD), part.dtype),
        grid_spec=pltpu.PrefetchScalarGridSpec(
            num_scalar_prefetch=1,
            grid=(1,),
            in_specs=[ANY],
            out_specs=ANY,
            scratch_shapes=[
                pltpu.VMEM(part.shape, part.dtype),
                pltpu.SemaphoreType.DMA((groups,)),
                pltpu.SemaphoreType.DMA((local, groups)),
            ],
        ),
        cost_estimate=pl.CostEstimate(
            flops=0, bytes_accessed=4 * groups * local * rows * HD, transcendentals=0
        ),
        name="unpack",
    )(swap, part)


def attend_kernel(tile, per_slab, plan, outs_at, count, idx_ref, live_ref, *refs):
    sources, refs = refs[:count], refs[count:]
    o_ref, held, q_held, o_held, s_held, sems, o_sems = refs[-7:]
    heads = len(plan)
    blocks, rows = sources[0].shape[0], sources[0].shape[2]
    slab = blocks * rows
    copies = []
    for h, taken in enumerate(plan):
        for at, parts in enumerate(taken):
            for n, (source, part) in enumerate(parts):
                into = q_held.at[h] if at == 0 else held.at[h, n, pl.ds((at - 1) * blocks, blocks)]
                copy = pltpu.make_async_copy(sources[source].at[:, part], into, sems.at[h, at, n])
                copy.start()
                copies.append((h, copy))
    flat = held.reshape(heads, 2, held.shape[2] * rows, HD)
    q_flat = q_held.reshape(heads, slab, HD)
    o_flat = o_held.reshape(heads, slab, HD)
    slots = idx_ref.shape[1]
    spans = tile // HD
    block = tile // PIECES

    begins = [[pl.multiple_of(idx_ref[t, j] * tile, 128) for j in range(slots)] for t in range(per_slab)]
    alive = [[live_ref[t, j] > 0 for j in range(slots)] for t in range(per_slab)]
    items = [(h, t, p) for h in range(heads) for t in range(per_slab) for p in range(PIECES)]

    def score(n, j, most):
        h, t, p = items[n]
        q = q_flat[h, pl.ds(t * tile + p * block, block), :]
        k = flat[h, 0, pl.ds(begins[t][j], tile), :]
        s = lax.dot_general(q, k, (((1,), (1,)), ((), ())), preferred_element_type=jnp.float32)
        s_held[n % 2, j] = s
        top = functools.reduce(jnp.maximum, [s[:, c * HD : (c + 1) * HD] for c in range(spans)])
        if j:
            top = jnp.where(alive[t][j], top, -jnp.inf)
        return top if most is None else jnp.maximum(most, top)

    def mix(n, j, top, total, mixed):
        h, t, _ = items[n]
        shift = jnp.where(alive[t][j], top, jnp.inf) if j else top
        expo = jnp.exp2(s_held[n % 2, j] * SCALE2 - shift)
        part = functools.reduce(jnp.add, [expo[:, c * HD : (c + 1) * HD] for c in range(spans)])
        v = flat[h, 1, pl.ds(begins[t][j], tile), :]
        pv = jnp.dot(expo.astype(jnp.bfloat16), v, preferred_element_type=jnp.float32)
        return (part, pv) if total is None else (total + part, mixed + pv)

    def arrive(head):
        for h, copy in copies:
            if h == head:
                copy.wait()

    arrive(0)
    most = None
    for j in range(slots):
        most = score(0, j, most)
    outs = []
    for n, (h, t, p) in enumerate(items):
        if n + 1 < len(items) and items[n + 1][0] != h:
            arrive(h + 1)
        top = jnp.max(most, axis=1, keepdims=True) * SCALE2
        most = total = mixed = None
        for j in range(slots):
            if n + 1 < len(items):
                most = score(n + 1, j, most)
            total, mixed = mix(n, j, top, total, mixed)
        total = jnp.sum(total, axis=1, keepdims=True)
        o_flat[h, pl.ds(t * tile + p * block, block), :] = (mixed / total).astype(o_flat.dtype)
        if t == per_slab - 1 and p == PIECES - 1:
            copy = pltpu.make_async_copy(o_held.at[h], o_ref.at[:, outs_at[h]], o_sems.at[h])
            copy.start()
            outs.append(copy)
    for copy in outs:
        copy.wait()


def attend(idx, live, sources, plan, outs_at, parts, into=None):
    per_slab, slots = idx.shape
    blocks, _, rows, _ = sources[0].shape
    slab = blocks * rows
    tile = slab // per_slab
    keys = slots * tile
    heads, columns = len(plan), len(plan[0]) - 1
    dtype = sources[0].dtype
    count = len(sources)
    held = [] if into is None else [into]
    return pl.pallas_call(
        functools.partial(attend_kernel, tile, per_slab, plan, outs_at, count),
        out_shape=jax.ShapeDtypeStruct((blocks, parts, rows, HD), dtype),
        grid_spec=pltpu.PrefetchScalarGridSpec(
            num_scalar_prefetch=2,
            grid=(1,),
            in_specs=[ANY] * (count + len(held)),
            out_specs=ANY,
            scratch_shapes=[
                pltpu.VMEM((heads, 2, columns * blocks, rows, HD), dtype),
                pltpu.VMEM((heads, blocks, rows, HD), dtype),
                pltpu.VMEM((heads, blocks, rows, HD), dtype),
                pltpu.VMEM((2, slots, tile // PIECES, tile), jnp.float32),
                pltpu.SemaphoreType.DMA((heads, columns + 1, 2)),
                pltpu.SemaphoreType.DMA((heads,)),
            ],
        ),
        input_output_aliases={2 + count: 0} if held else {},
        cost_estimate=pl.CostEstimate(
            flops=4 * heads * slab * keys * HD,
            bytes_accessed=4 * heads * slab * HD * (columns + 1),
            transcendentals=heads * slab * keys,
        ),
        name="attend",
    )(idx, live, *sources, *held)


def body(query, keys, values, windows):
    groups = lax.axis_size("head")
    peers = lax.axis_size("seq")
    columns = peers // TFR
    local = query.shape[1] // (groups * HD)
    per_slab = windows.shape[0]

    across = [(s, s ^ columns) for s in range(peers)]
    right = [(s, s + 1) for s in range(peers) if (s + 1) % columns]
    left = [(s, s - 1) for s in range(peers) if s % columns]
    middle = [(s, s + 2 * columns) for s in range(columns)] + [
        (s, s - 2 * columns) for s in range(3 * columns, peers)
    ]

    def send(x, pairs):
        return lax.ppermute(x, "seq", pairs)

    def exchange(x):
        return lax.all_to_all(x, "head", split_axis=0, concat_axis=0, tiled=True)

    here = lax.axis_index("seq")
    live = windows >= 0
    delta = windows // per_slab - here
    partner = jnp.where(here // columns % 2 == 0, columns, -columns)
    code = jnp.where(
        delta == 0,
        0,
        jnp.where(delta == -1, 1, jnp.where(delta == 1, 2, jnp.where(delta == partner, 3, 4))),
    )
    idx = jnp.where(live, code * per_slab + windows % per_slab, 0)
    live = live.astype(jnp.int32)

    swap = (here >= peers // 2).astype(jnp.int32).reshape(1)
    hop = [(s * groups + h, d * groups + (h ^ 1)) for s, d in middle for h in range(groups)]

    first = pack(swap, [keys, values], [(0, 0), (1, 0), (0, 1)], groups)
    crossed = send(first, across)
    rest = pack(swap, [keys, values], [(1, 1), (0, 2), (1, 2)], groups)
    rest = exchange(rest)
    most = pack(swap, [keys, values, query], [(2, 0), (2, 1), (2, 2), (0, 0), (1, 0), (0, 1)], groups)
    most = exchange(most)
    far_1 = send(rest[:, 0:1], across)
    far_2 = send(rest[:, 1:3], across)
    crossed = exchange(crossed)
    before_a = send(rest, right)
    behind_a = send(rest, left)
    own = most[:, 3:6]
    before_b = send(own, right)
    behind_b = send(own, left)
    second_2 = lax.ppermute(far_2, ("seq", "head"), hop)
    second_1 = send(far_1, middle)
    second_b = send(crossed, middle)
    parts = local
    plan_0 = [[((0, 0),), ((0, 3), (0, 4)), ((1, 0), (1, 1)), ((2, 0), (2, 1)), ((3, 0), (3, 1)), ((4, 0), (4, 1))]]
    o = attend(idx, live, [most, before_b, behind_b, crossed, second_b], plan_0, (0,), parts)
    sources = [most, rest, before_a, behind_a, far_1, second_1, before_b, behind_b, crossed, second_b, second_2, far_2]
    plan = [
        [((0, 1),), ((0, 5), (1, 0)), ((6, 2), (2, 0)), ((7, 2), (3, 0)), ((8, 2), (4, 0)), ((9, 2), (5, 0))],
        [((0, 2),), ((1, 1), (1, 2)), ((2, 1), (2, 2)), ((3, 1), (3, 2)), ((11, 0), (11, 1)), ((10, 0), (10, 1))],
    ]
    o = attend(idx, live, sources, plan, (1, 2), parts, o)
    o = exchange(o)
    return unpack(swap, o)


def solution(mesh):
    return jax.shard_map(
        body,
        mesh=mesh,
        in_specs=(
            P(("seq", "head"), None),
            P(("seq", "head"), None),
            P(("seq", "head"), None),
            P("seq", None),
        ),
        out_specs=P(("seq", "head"), None),
        check_vma=False,
    )
```

```python
import functools

import jax
import jax.numpy as jnp
from jax import lax
from jax.experimental import pallas as pl
from jax.experimental.pallas import tpu as pltpu
from jax.sharding import PartitionSpec as P


HD = 128
TFR = 4
PIECES = 1
SWAPPED = 2
SCALE2 = 1.4426950408889634 / HD**0.5


ANY = pl.BlockSpec(memory_space=pl.ANY)


def after(value, *first):
    return lax.optimization_barrier((value,) + first)[0]


def lane(g, head, local, swap):
    return pl.multiple_of(((g if swap is None else jnp.bitwise_xor(g, swap)) * local + head) * HD, HD)


def pack_kernel(picks, local, count, swap_ref, *refs):
    arrays, o_ref, sems = refs[:count], refs[count], refs[count + 1]
    copies = []
    for at, (array, head) in enumerate(picks):
        swap = swap_ref[0] if head == SWAPPED else None
        for g in range(o_ref.shape[0]):
            piece = arrays[array].at[:, pl.ds(lane(g, head, local, swap), HD)]
            copy = pltpu.make_async_copy(piece, o_ref.at[g, at], sems.at[at, g])
            copy.start()
            copies.append(copy)
    for copy in copies:
        copy.wait()


def pack(swap, arrays, picks, groups):
    rows, width = arrays[0].shape
    shape = (groups, len(picks), rows, HD)
    return pl.pallas_call(
        functools.partial(pack_kernel, picks, width // (groups * HD), len(arrays)),
        out_shape=jax.ShapeDtypeStruct(shape, arrays[0].dtype),
        grid_spec=pltpu.PrefetchScalarGridSpec(
            num_scalar_prefetch=1,
            grid=(1,),
            in_specs=[ANY] * len(arrays),
            out_specs=pl.BlockSpec(shape, lambda i, *_: (0, 0, 0, 0)),
            scratch_shapes=[pltpu.SemaphoreType.DMA((len(picks), groups))],
        ),
        cost_estimate=pl.CostEstimate(
            flops=0, bytes_accessed=4 * groups * len(picks) * rows * HD, transcendentals=0
        ),
        name="pack",
    )(swap, *arrays)


def unpack_kernel(swap_ref, part, o_ref, held, in_sems, sems):
    groups, local = part.shape[:2]
    arriving, leaving = [], []
    for g in range(groups):
        copy = pltpu.make_async_copy(part.at[g], held.at[g], in_sems.at[g])
        copy.start()
        arriving.append(copy)
    for g in range(groups):
        arriving[g].wait()
        for head in range(local):
            swap = swap_ref[0] if head == SWAPPED else None
            copy = pltpu.make_async_copy(
                held.at[g, head], o_ref.at[:, pl.ds(lane(g, head, local, swap), HD)], sems.at[head, g]
            )
            copy.start()
            leaving.append(copy)
    for copy in leaving:
        copy.wait()


def unpack(swap, part):
    groups, local, rows, _ = part.shape
    return pl.pallas_call(
        unpack_kernel,
        out_shape=jax.ShapeDtypeStruct((rows, groups * local * HD), part.dtype),
        grid_spec=pltpu.PrefetchScalarGridSpec(
            num_scalar_prefetch=1,
            grid=(1,),
            in_specs=[ANY],
            out_specs=ANY,
            scratch_shapes=[
                pltpu.VMEM(part.shape, part.dtype),
                pltpu.SemaphoreType.DMA((groups,)),
                pltpu.SemaphoreType.DMA((local, groups)),
            ],
        ),
        cost_estimate=pl.CostEstimate(
            flops=0, bytes_accessed=4 * groups * local * rows * HD, transcendentals=0
        ),
        name="unpack",
    )(swap, part)


def attend_kernel(tile, per_slab, plan, outs_at, count, idx_ref, live_ref, *refs):
    sources, refs = refs[:count], refs[count:]
    o_ref, held, q_held, o_held, s_held, sems, o_sems = refs[-7:]
    heads = len(plan)
    blocks, rows = sources[0].shape[0], sources[0].shape[2]
    slab = blocks * rows
    copies = []
    for h, taken in enumerate(plan):
        for at, parts in enumerate(taken):
            for n, (source, part) in enumerate(parts):
                into = q_held.at[h] if at == 0 else held.at[h, n, pl.ds((at - 1) * blocks, blocks)]
                copy = pltpu.make_async_copy(sources[source].at[:, part], into, sems.at[h, at, n])
                copy.start()
                copies.append((h, copy))
    flat = held.reshape(heads, 2, held.shape[2] * rows, HD)
    q_flat = q_held.reshape(heads, slab, HD)
    o_flat = o_held.reshape(heads, slab, HD)
    slots = idx_ref.shape[1]
    spans = tile // HD
    block = tile // PIECES

    begins = [[pl.multiple_of(idx_ref[t, j] * tile, 128) for j in range(slots)] for t in range(per_slab)]
    alive = [[live_ref[t, j] > 0 for j in range(slots)] for t in range(per_slab)]
    items = [(h, t, p) for h in range(heads) for t in range(per_slab) for p in range(PIECES)]

    def score(n, j, most):
        h, t, p = items[n]
        q = q_flat[h, pl.ds(t * tile + p * block, block), :]
        k = flat[h, 0, pl.ds(begins[t][j], tile), :]
        s = lax.dot_general(q, k, (((1,), (1,)), ((), ())), preferred_element_type=jnp.float32)
        s_held[n % 2, j] = s
        top = functools.reduce(jnp.maximum, [s[:, c * HD : (c + 1) * HD] for c in range(spans)])
        if j:
            top = jnp.where(alive[t][j], top, -jnp.inf)
        return top if most is None else jnp.maximum(most, top)

    def mix(n, j, top, total, mixed):
        h, t, _ = items[n]
        shift = jnp.where(alive[t][j], top, jnp.inf) if j else top
        expo = jnp.exp2(s_held[n % 2, j] * SCALE2 - shift)
        part = functools.reduce(jnp.add, [expo[:, c * HD : (c + 1) * HD] for c in range(spans)])
        v = flat[h, 1, pl.ds(begins[t][j], tile), :]
        pv = jnp.dot(expo.astype(jnp.bfloat16), v, preferred_element_type=jnp.float32)
        return (part, pv) if total is None else (total + part, mixed + pv)

    def arrive(head):
        for h, copy in copies:
            if h == head:
                copy.wait()

    arrive(0)
    most = None
    for j in range(slots):
        most = score(0, j, most)
    outs = []
    for n, (h, t, p) in enumerate(items):
        if n + 1 < len(items) and items[n + 1][0] != h:
            arrive(h + 1)
        top = jnp.max(most, axis=1, keepdims=True) * SCALE2
        most = total = mixed = None
        for j in range(slots):
            if n + 1 < len(items):
                most = score(n + 1, j, most)
            total, mixed = mix(n, j, top, total, mixed)
        total = jnp.sum(total, axis=1, keepdims=True)
        o_flat[h, pl.ds(t * tile + p * block, block), :] = (mixed / total).astype(o_flat.dtype)
        if t == per_slab - 1 and p == PIECES - 1:
            copy = pltpu.make_async_copy(o_held.at[h], o_ref.at[:, outs_at[h]], o_sems.at[h])
            copy.start()
            outs.append(copy)
    for copy in outs:
        copy.wait()


def attend(idx, live, sources, plan, outs_at, parts, into=None):
    per_slab, slots = idx.shape
    blocks, _, rows, _ = sources[0].shape
    slab = blocks * rows
    tile = slab // per_slab
    keys = slots * tile
    heads, columns = len(plan), len(plan[0]) - 1
    dtype = sources[0].dtype
    count = len(sources)
    held = [] if into is None else [into]
    return pl.pallas_call(
        functools.partial(attend_kernel, tile, per_slab, plan, outs_at, count),
        out_shape=jax.ShapeDtypeStruct((blocks, parts, rows, HD), dtype),
        grid_spec=pltpu.PrefetchScalarGridSpec(
            num_scalar_prefetch=2,
            grid=(1,),
            in_specs=[ANY] * (count + len(held)),
            out_specs=ANY,
            scratch_shapes=[
                pltpu.VMEM((heads, 2, columns * blocks, rows, HD), dtype),
                pltpu.VMEM((heads, blocks, rows, HD), dtype),
                pltpu.VMEM((heads, blocks, rows, HD), dtype),
                pltpu.VMEM((2, slots, tile // PIECES, tile), jnp.float32),
                pltpu.SemaphoreType.DMA((heads, columns + 1, 2)),
                pltpu.SemaphoreType.DMA((heads,)),
            ],
        ),
        input_output_aliases={2 + count: 0} if held else {},
        cost_estimate=pl.CostEstimate(
            flops=4 * heads * slab * keys * HD,
            bytes_accessed=4 * heads * slab * HD * (columns + 1),
            transcendentals=heads * slab * keys,
        ),
        name="attend",
    )(idx, live, *sources, *held)


def body(query, keys, values, windows):
    groups = lax.axis_size("head")
    peers = lax.axis_size("seq")
    columns = peers // TFR
    local = query.shape[1] // (groups * HD)
    per_slab = windows.shape[0]

    across = [(s, s ^ columns) for s in range(peers)]
    right = [(s, s + 1) for s in range(peers) if (s + 1) % columns]
    left = [(s, s - 1) for s in range(peers) if s % columns]
    middle = [(s, s + 2 * columns) for s in range(columns)] + [
        (s, s - 2 * columns) for s in range(3 * columns, peers)
    ]

    def send(x, pairs):
        return lax.ppermute(x, "seq", pairs)

    def exchange(x):
        return lax.all_to_all(x, "head", split_axis=0, concat_axis=0, tiled=True)

    here = lax.axis_index("seq")
    live = windows >= 0
    delta = windows // per_slab - here
    partner = jnp.where(here // columns % 2 == 0, columns, -columns)
    code = jnp.where(
        delta == 0,
        0,
        jnp.where(delta == -1, 1, jnp.where(delta == 1, 2, jnp.where(delta == partner, 3, 4))),
    )
    idx = jnp.where(live, code * per_slab + windows % per_slab, 0)
    live = live.astype(jnp.int32)

    swap = (here >= peers // 2).astype(jnp.int32).reshape(1)
    hop = [(s * groups + h, d * groups + (h ^ 1)) for s, d in middle for h in range(groups)]

    first = pack(swap, [keys, values], [(0, 0), (1, 0), (0, 1)], groups)
    crossed = send(first, across)
    rest = pack(swap, [keys, values], [(1, 1), (0, 2), (1, 2)], groups)
    rest = exchange(rest)
    own = exchange(first)
    most = pack(swap, [query], [(0, 0), (0, 1), (0, 2)], groups)
    far_1 = send(rest[:, 0:1], across)
    far_2 = send(after(rest[:, 1:3], crossed), across)
    crossed = exchange(crossed)
    most = exchange(most)
    before_a = send(rest, right)
    behind_a = send(rest, left)
    before_b = send(own, right)
    behind_b = send(own, left)
    second_2 = lax.ppermute(far_2, ("seq", "head"), hop)
    second_1 = send(far_1, middle)
    second_b = send(crossed, middle)
    parts = local
    plan_0 = [[((0, 0),)] + [((n, 0), (n, 1)) for n in range(1, 6)]]
    o = attend(idx, live, [most, own, before_b, behind_b, crossed, second_b], plan_0, (0,), parts)
    sources = [most, rest, before_a, behind_a, far_1, second_1, before_b, behind_b, crossed, second_b, second_2, far_2, own]
    plan = [
        [((0, 1),), ((12, 2), (1, 0)), ((6, 2), (2, 0)), ((7, 2), (3, 0)), ((8, 2), (4, 0)), ((9, 2), (5, 0))],
        [((0, 2),), ((1, 1), (1, 2)), ((2, 1), (2, 2)), ((3, 1), (3, 2)), ((11, 0), (11, 1)), ((10, 0), (10, 1))],
    ]
    o = attend(idx, live, sources, plan, (1, 2), parts, o)
    o = exchange(o)
    return unpack(swap, o)


def solution(mesh):
    return jax.shard_map(
        body,
        mesh=mesh,
        in_specs=(
            P(("seq", "head"), None),
            P(("seq", "head"), None),
            P(("seq", "head"), None),
            P("seq", None),
        ),
        out_specs=P(("seq", "head"), None),
        check_vma=False,
    )
```

```python
import functools

import jax
import jax.numpy as jnp
from jax import lax
from jax.experimental import pallas as pl
from jax.experimental.pallas import tpu as pltpu
from jax.sharding import PartitionSpec as P


HD = 128
TFR = 4
PIECES = 1
SWAPPED = 2
SCALE2 = 1.4426950408889634 / HD**0.5


ANY = pl.BlockSpec(memory_space=pl.ANY)


def after(value, *first):
    return lax.optimization_barrier((value,) + first)[0]


def lane(g, head, local, swap):
    return pl.multiple_of(((g if swap is None else jnp.bitwise_xor(g, swap)) * local + head) * HD, HD)


def pack_kernel(picks, local, count, swap_ref, *refs):
    arrays, o_ref, sems = refs[:count], refs[count], refs[count + 1]
    copies = []
    for at, (array, head) in enumerate(picks):
        swap = swap_ref[0] if head == SWAPPED else None
        for g in range(o_ref.shape[0]):
            piece = arrays[array].at[:, pl.ds(lane(g, head, local, swap), HD)]
            copy = pltpu.make_async_copy(piece, o_ref.at[g, at], sems.at[at, g])
            copy.start()
            copies.append(copy)
    for copy in copies:
        copy.wait()


def pack(swap, arrays, picks, groups):
    rows, width = arrays[0].shape
    shape = (groups, len(picks), rows, HD)
    return pl.pallas_call(
        functools.partial(pack_kernel, picks, width // (groups * HD), len(arrays)),
        out_shape=jax.ShapeDtypeStruct(shape, arrays[0].dtype),
        grid_spec=pltpu.PrefetchScalarGridSpec(
            num_scalar_prefetch=1,
            grid=(1,),
            in_specs=[ANY] * len(arrays),
            out_specs=pl.BlockSpec(shape, lambda i, *_: (0, 0, 0, 0)),
            scratch_shapes=[pltpu.SemaphoreType.DMA((len(picks), groups))],
        ),
        cost_estimate=pl.CostEstimate(
            flops=0, bytes_accessed=4 * groups * len(picks) * rows * HD, transcendentals=0
        ),
        name="pack",
    )(swap, *arrays)


def unpack_kernel(swap_ref, part, o_ref, held, in_sems, sems):
    groups, local = part.shape[:2]
    arriving, leaving = [], []
    for g in range(groups):
        copy = pltpu.make_async_copy(part.at[g], held.at[g], in_sems.at[g])
        copy.start()
        arriving.append(copy)
    for g in range(groups):
        arriving[g].wait()
        for head in range(local):
            swap = swap_ref[0] if head == SWAPPED else None
            copy = pltpu.make_async_copy(
                held.at[g, head], o_ref.at[:, pl.ds(lane(g, head, local, swap), HD)], sems.at[head, g]
            )
            copy.start()
            leaving.append(copy)
    for copy in leaving:
        copy.wait()


def unpack(swap, part):
    groups, local, rows, _ = part.shape
    return pl.pallas_call(
        unpack_kernel,
        out_shape=jax.ShapeDtypeStruct((rows, groups * local * HD), part.dtype),
        grid_spec=pltpu.PrefetchScalarGridSpec(
            num_scalar_prefetch=1,
            grid=(1,),
            in_specs=[ANY],
            out_specs=ANY,
            scratch_shapes=[
                pltpu.VMEM(part.shape, part.dtype),
                pltpu.SemaphoreType.DMA((groups,)),
                pltpu.SemaphoreType.DMA((local, groups)),
            ],
        ),
        cost_estimate=pl.CostEstimate(
            flops=0, bytes_accessed=4 * groups * local * rows * HD, transcendentals=0
        ),
        name="unpack",
    )(swap, part)


def attend_kernel(tile, per_slab, plan, outs_at, count, idx_ref, live_ref, *refs):
    sources, refs = refs[:count], refs[count:]
    o_ref, held, q_held, o_held, s_held, sems, o_sems = refs[-7:]
    heads = len(plan)
    blocks, rows = sources[0].shape[0], sources[0].shape[2]
    slab = blocks * rows
    copies = []
    for h, taken in enumerate(plan):
        for at, parts in enumerate(taken):
            for n, (source, part) in enumerate(parts):
                into = q_held.at[h] if at == 0 else held.at[h, n, pl.ds((at - 1) * blocks, blocks)]
                copy = pltpu.make_async_copy(sources[source].at[:, part], into, sems.at[h, at, n])
                copy.start()
                copies.append((h, copy))
    flat = held.reshape(heads, 2, held.shape[2] * rows, HD)
    q_flat = q_held.reshape(heads, slab, HD)
    o_flat = o_held.reshape(heads, slab, HD)
    slots = idx_ref.shape[1]
    spans = tile // HD
    block = tile // PIECES

    begins = [[pl.multiple_of(idx_ref[t, j] * tile, 128) for j in range(slots)] for t in range(per_slab)]
    alive = [[live_ref[t, j] > 0 for j in range(slots)] for t in range(per_slab)]
    items = [(h, t, p) for h in range(heads) for t in range(per_slab) for p in range(PIECES)]

    def score(n, j, most):
        h, t, p = items[n]
        q = q_flat[h, pl.ds(t * tile + p * block, block), :]
        k = flat[h, 0, pl.ds(begins[t][j], tile), :]
        s = lax.dot_general(q, k, (((1,), (1,)), ((), ())), preferred_element_type=jnp.float32)
        s_held[n % 2, j] = s
        top = functools.reduce(jnp.maximum, [s[:, c * HD : (c + 1) * HD] for c in range(spans)])
        if j:
            top = jnp.where(alive[t][j], top, -jnp.inf)
        return top if most is None else jnp.maximum(most, top)

    def mix(n, j, top, total, mixed):
        h, t, _ = items[n]
        shift = jnp.where(alive[t][j], top, jnp.inf) if j else top
        expo = jnp.exp2(s_held[n % 2, j] * SCALE2 - shift)
        part = functools.reduce(jnp.add, [expo[:, c * HD : (c + 1) * HD] for c in range(spans)])
        v = flat[h, 1, pl.ds(begins[t][j], tile), :]
        pv = jnp.dot(expo.astype(jnp.bfloat16), v, preferred_element_type=jnp.float32)
        return (part, pv) if total is None else (total + part, mixed + pv)

    def arrive(head):
        for h, copy in copies:
            if h == head:
                copy.wait()

    arrive(0)
    most = None
    for j in range(slots):
        most = score(0, j, most)
    outs = []
    for n, (h, t, p) in enumerate(items):
        if n + 1 < len(items) and items[n + 1][0] != h:
            arrive(h + 1)
        top = jnp.max(most, axis=1, keepdims=True) * SCALE2
        most = total = mixed = None
        for j in range(slots):
            if n + 1 < len(items):
                most = score(n + 1, j, most)
            total, mixed = mix(n, j, top, total, mixed)
        total = jnp.sum(total, axis=1, keepdims=True)
        o_flat[h, pl.ds(t * tile + p * block, block), :] = (mixed / total).astype(o_flat.dtype)
        if t == per_slab - 1 and p == PIECES - 1:
            copy = pltpu.make_async_copy(o_held.at[h], o_ref.at[:, outs_at[h]], o_sems.at[h])
            copy.start()
            outs.append(copy)
    for copy in outs:
        copy.wait()


def attend(idx, live, sources, plan, outs_at, parts, into=None):
    per_slab, slots = idx.shape
    blocks, _, rows, _ = sources[0].shape
    slab = blocks * rows
    tile = slab // per_slab
    keys = slots * tile
    heads, columns = len(plan), len(plan[0]) - 1
    dtype = sources[0].dtype
    count = len(sources)
    held = [] if into is None else [into]
    return pl.pallas_call(
        functools.partial(attend_kernel, tile, per_slab, plan, outs_at, count),
        out_shape=jax.ShapeDtypeStruct((blocks, parts, rows, HD), dtype),
        grid_spec=pltpu.PrefetchScalarGridSpec(
            num_scalar_prefetch=2,
            grid=(1,),
            in_specs=[ANY] * (count + len(held)),
            out_specs=ANY,
            scratch_shapes=[
                pltpu.VMEM((heads, 2, columns * blocks, rows, HD), dtype),
                pltpu.VMEM((heads, blocks, rows, HD), dtype),
                pltpu.VMEM((heads, blocks, rows, HD), dtype),
                pltpu.VMEM((2, slots, tile // PIECES, tile), jnp.float32),
                pltpu.SemaphoreType.DMA((heads, columns + 1, 2)),
                pltpu.SemaphoreType.DMA((heads,)),
            ],
        ),
        input_output_aliases={2 + count: 0} if held else {},
        cost_estimate=pl.CostEstimate(
            flops=4 * heads * slab * keys * HD,
            bytes_accessed=4 * heads * slab * HD * (columns + 1),
            transcendentals=heads * slab * keys,
        ),
        name="attend",
    )(idx, live, *sources, *held)


def body(query, keys, values, windows):
    groups = lax.axis_size("head")
    peers = lax.axis_size("seq")
    columns = peers // TFR
    local = query.shape[1] // (groups * HD)
    per_slab = windows.shape[0]

    across = [(s, s ^ columns) for s in range(peers)]
    right = [(s, s + 1) for s in range(peers) if (s + 1) % columns]
    left = [(s, s - 1) for s in range(peers) if s % columns]
    middle = [(s, s + 2 * columns) for s in range(columns)] + [
        (s, s - 2 * columns) for s in range(3 * columns, peers)
    ]

    def send(x, pairs):
        return lax.ppermute(x, "seq", pairs)

    def exchange(x):
        return lax.all_to_all(x, "head", split_axis=0, concat_axis=0, tiled=True)

    here = lax.axis_index("seq")
    live = windows >= 0
    delta = windows // per_slab - here
    partner = jnp.where(here // columns % 2 == 0, columns, -columns)
    code = jnp.where(
        delta == 0,
        0,
        jnp.where(delta == -1, 1, jnp.where(delta == 1, 2, jnp.where(delta == partner, 3, 4))),
    )
    idx = jnp.where(live, code * per_slab + windows % per_slab, 0)
    live = live.astype(jnp.int32)

    swap = (here >= peers // 2).astype(jnp.int32).reshape(1)
    hop = [(s * groups + h, d * groups + (h ^ 1)) for s, d in middle for h in range(groups)]

    first = pack(swap, [keys, values], [(0, 0), (1, 0), (0, 1)], groups)
    crossed = send(first, across)
    rest = pack(swap, [keys, values], [(1, 1), (0, 2), (1, 2)], groups)
    rest = exchange(rest)
    most = pack(swap, [keys, values, query], [(2, 0), (2, 1), (2, 2), (0, 0), (1, 0), (0, 1)], groups)
    most = exchange(most)
    far_1 = send(after(rest[:, 0:1], crossed), across)
    far_2 = send(after(rest[:, 1:3], crossed), across)
    crossed = exchange(crossed)
    before_a = send(rest, right)
    behind_a = send(rest, left)
    own = most[:, 3:6]
    before_b = send(own, right)
    behind_b = send(own, left)
    second_2 = lax.ppermute(far_2, ("seq", "head"), hop)
    second_1 = send(far_1, middle)
    second_b = send(crossed, middle)
    parts = local
    plan_0 = [[((0, 0),), ((0, 3), (0, 4)), ((1, 0), (1, 1)), ((2, 0), (2, 1)), ((3, 0), (3, 1)), ((4, 0), (4, 1))]]
    o = attend(idx, live, [most, before_b, behind_b, crossed, second_b], plan_0, (0,), parts)
    sources = [most, rest, before_a, behind_a, far_1, second_1, before_b, behind_b, crossed, second_b, second_2, far_2]
    plan = [
        [((0, 1),), ((0, 5), (1, 0)), ((6, 2), (2, 0)), ((7, 2), (3, 0)), ((8, 2), (4, 0)), ((9, 2), (5, 0))],
        [((0, 2),), ((1, 1), (1, 2)), ((2, 1), (2, 2)), ((3, 1), (3, 2)), ((11, 0), (11, 1)), ((10, 0), (10, 1))],
    ]
    o = attend(idx, live, sources, plan, (1, 2), parts, o)
    o = exchange(o)
    return unpack(swap, o)


def solution(mesh):
    return jax.shard_map(
        body,
        mesh=mesh,
        in_specs=(
            P(("seq", "head"), None),
            P(("seq", "head"), None),
            P(("seq", "head"), None),
            P("seq", None),
        ),
        out_specs=P(("seq", "head"), None),
        check_vma=False,
    )
```

```python
import functools

import jax
import jax.numpy as jnp
from jax import lax
from jax.experimental import pallas as pl
from jax.experimental.pallas import tpu as pltpu
from jax.sharding import PartitionSpec as P


HD = 128
TFR = 4
PIECES = 1
SWAPPED = 2
SCALE2 = 1.4426950408889634 / HD**0.5


ANY = pl.BlockSpec(memory_space=pl.ANY)


def after(value, *first):
    return lax.optimization_barrier((value,) + first)[0]


def lane(g, head, local, swap):
    return pl.multiple_of(((g if swap is None else jnp.bitwise_xor(g, swap)) * local + head) * HD, HD)


def pack_kernel(picks, local, count, swap_ref, *refs):
    arrays, o_ref, sems = refs[:count], refs[count], refs[count + 1]
    copies = []
    for at, (array, head) in enumerate(picks):
        swap = swap_ref[0] if head == SWAPPED else None
        for g in range(o_ref.shape[0]):
            piece = arrays[array].at[:, pl.ds(lane(g, head, local, swap), HD)]
            copy = pltpu.make_async_copy(piece, o_ref.at[g, at], sems.at[at, g])
            copy.start()
            copies.append(copy)
    for copy in copies:
        copy.wait()


def pack(swap, arrays, picks, groups):
    rows, width = arrays[0].shape
    shape = (groups, len(picks), rows, HD)
    return pl.pallas_call(
        functools.partial(pack_kernel, picks, width // (groups * HD), len(arrays)),
        out_shape=jax.ShapeDtypeStruct(shape, arrays[0].dtype),
        grid_spec=pltpu.PrefetchScalarGridSpec(
            num_scalar_prefetch=1,
            grid=(1,),
            in_specs=[ANY] * len(arrays),
            out_specs=pl.BlockSpec(shape, lambda i, *_: (0, 0, 0, 0)),
            scratch_shapes=[pltpu.SemaphoreType.DMA((len(picks), groups))],
        ),
        cost_estimate=pl.CostEstimate(
            flops=0, bytes_accessed=4 * groups * len(picks) * rows * HD, transcendentals=0
        ),
        name="pack",
    )(swap, *arrays)


def unpack_kernel(swap_ref, part, o_ref, held, in_sems, sems):
    groups, local = part.shape[:2]
    arriving, leaving = [], []
    for g in range(groups):
        copy = pltpu.make_async_copy(part.at[g], held.at[g], in_sems.at[g])
        copy.start()
        arriving.append(copy)
    for g in range(groups):
        arriving[g].wait()
        for head in range(local):
            swap = swap_ref[0] if head == SWAPPED else None
            copy = pltpu.make_async_copy(
                held.at[g, head], o_ref.at[:, pl.ds(lane(g, head, local, swap), HD)], sems.at[head, g]
            )
            copy.start()
            leaving.append(copy)
    for copy in leaving:
        copy.wait()


def unpack(swap, part):
    groups, local, rows, _ = part.shape
    return pl.pallas_call(
        unpack_kernel,
        out_shape=jax.ShapeDtypeStruct((rows, groups * local * HD), part.dtype),
        grid_spec=pltpu.PrefetchScalarGridSpec(
            num_scalar_prefetch=1,
            grid=(1,),
            in_specs=[ANY],
            out_specs=ANY,
            scratch_shapes=[
                pltpu.VMEM(part.shape, part.dtype),
                pltpu.SemaphoreType.DMA((groups,)),
                pltpu.SemaphoreType.DMA((local, groups)),
            ],
        ),
        cost_estimate=pl.CostEstimate(
            flops=0, bytes_accessed=4 * groups * local * rows * HD, transcendentals=0
        ),
        name="unpack",
    )(swap, part)


def attend_kernel(tile, per_slab, plan, outs_at, count, idx_ref, live_ref, *refs):
    sources, refs = refs[:count], refs[count:]
    o_ref, held, q_held, o_held, s_held, sems, o_sems = refs[-7:]
    heads = len(plan)
    blocks, rows = sources[0].shape[0], sources[0].shape[2]
    slab = blocks * rows
    copies = []
    for h, taken in enumerate(plan):
        for at, parts in enumerate(taken):
            for n, (source, part) in enumerate(parts):
                into = q_held.at[h] if at == 0 else held.at[h, n, pl.ds((at - 1) * blocks, blocks)]
                copy = pltpu.make_async_copy(sources[source].at[:, part], into, sems.at[h, at, n])
                copy.start()
                copies.append((h, copy))
    flat = held.reshape(heads, 2, held.shape[2] * rows, HD)
    q_flat = q_held.reshape(heads, slab, HD)
    o_flat = o_held.reshape(heads, slab, HD)
    slots = idx_ref.shape[1]
    spans = tile // HD
    block = tile // PIECES

    begins = [[pl.multiple_of(idx_ref[t, j] * tile, 128) for j in range(slots)] for t in range(per_slab)]
    alive = [[live_ref[t, j] > 0 for j in range(slots)] for t in range(per_slab)]
    items = [(h, t, p) for h in range(heads) for t in range(per_slab) for p in range(PIECES)]

    def score(n, j, most):
        h, t, p = items[n]
        q = q_flat[h, pl.ds(t * tile + p * block, block), :]
        k = flat[h, 0, pl.ds(begins[t][j], tile), :]
        s = lax.dot_general(q, k, (((1,), (1,)), ((), ())), preferred_element_type=jnp.float32)
        s_held[n % 2, j] = s
        top = functools.reduce(jnp.maximum, [s[:, c * HD : (c + 1) * HD] for c in range(spans)])
        if j:
            top = jnp.where(alive[t][j], top, -jnp.inf)
        return top if most is None else jnp.maximum(most, top)

    def mix(n, j, top, total, mixed):
        h, t, _ = items[n]
        shift = jnp.where(alive[t][j], top, jnp.inf) if j else top
        expo = jnp.exp2(s_held[n % 2, j] * SCALE2 - shift)
        part = functools.reduce(jnp.add, [expo[:, c * HD : (c + 1) * HD] for c in range(spans)])
        v = flat[h, 1, pl.ds(begins[t][j], tile), :]
        pv = jnp.dot(expo.astype(jnp.bfloat16), v, preferred_element_type=jnp.float32)
        return (part, pv) if total is None else (total + part, mixed + pv)

    def arrive(head):
        for h, copy in copies:
            if h == head:
                copy.wait()

    arrive(0)
    most = None
    for j in range(slots):
        most = score(0, j, most)
    outs = []
    for n, (h, t, p) in enumerate(items):
        if n + 1 < len(items) and items[n + 1][0] != h:
            arrive(h + 1)
        top = jnp.max(most, axis=1, keepdims=True) * SCALE2
        most = total = mixed = None
        for j in range(slots):
            if n + 1 < len(items):
                most = score(n + 1, j, most)
            total, mixed = mix(n, j, top, total, mixed)
        total = jnp.sum(total, axis=1, keepdims=True)
        o_flat[h, pl.ds(t * tile + p * block, block), :] = (mixed / total).astype(o_flat.dtype)
        if t == per_slab - 1 and p == PIECES - 1:
            copy = pltpu.make_async_copy(o_held.at[h], o_ref.at[:, outs_at[h]], o_sems.at[h])
            copy.start()
            outs.append(copy)
    for copy in outs:
        copy.wait()


def attend(idx, live, sources, plan, outs_at, parts, into=None):
    per_slab, slots = idx.shape
    blocks, _, rows, _ = sources[0].shape
    slab = blocks * rows
    tile = slab // per_slab
    keys = slots * tile
    heads, columns = len(plan), len(plan[0]) - 1
    dtype = sources[0].dtype
    count = len(sources)
    held = [] if into is None else [into]
    return pl.pallas_call(
        functools.partial(attend_kernel, tile, per_slab, plan, outs_at, count),
        out_shape=jax.ShapeDtypeStruct((blocks, parts, rows, HD), dtype),
        grid_spec=pltpu.PrefetchScalarGridSpec(
            num_scalar_prefetch=2,
            grid=(1,),
            in_specs=[ANY] * (count + len(held)),
            out_specs=ANY,
            scratch_shapes=[
                pltpu.VMEM((heads, 2, columns * blocks, rows, HD), dtype),
                pltpu.VMEM((heads, blocks, rows, HD), dtype),
                pltpu.VMEM((heads, blocks, rows, HD), dtype),
                pltpu.VMEM((2, slots, tile // PIECES, tile), jnp.float32),
                pltpu.SemaphoreType.DMA((heads, columns + 1, 2)),
                pltpu.SemaphoreType.DMA((heads,)),
            ],
        ),
        input_output_aliases={2 + count: 0} if held else {},
        cost_estimate=pl.CostEstimate(
            flops=4 * heads * slab * keys * HD,
            bytes_accessed=4 * heads * slab * HD * (columns + 1),
            transcendentals=heads * slab * keys,
        ),
        name="attend",
    )(idx, live, *sources, *held)


def body(query, keys, values, windows):
    groups = lax.axis_size("head")
    peers = lax.axis_size("seq")
    columns = peers // TFR
    local = query.shape[1] // (groups * HD)
    per_slab = windows.shape[0]

    across = [(s, s ^ columns) for s in range(peers)]
    right = [(s, s + 1) for s in range(peers) if (s + 1) % columns]
    left = [(s, s - 1) for s in range(peers) if s % columns]
    middle = [(s, s + 2 * columns) for s in range(columns)] + [
        (s, s - 2 * columns) for s in range(3 * columns, peers)
    ]

    def send(x, pairs):
        return lax.ppermute(x, "seq", pairs)

    def exchange(x):
        return lax.all_to_all(x, "head", split_axis=0, concat_axis=0, tiled=True)

    here = lax.axis_index("seq")
    live = windows >= 0
    delta = windows // per_slab - here
    partner = jnp.where(here // columns % 2 == 0, columns, -columns)
    code = jnp.where(
        delta == 0,
        0,
        jnp.where(delta == -1, 1, jnp.where(delta == 1, 2, jnp.where(delta == partner, 3, 4))),
    )
    idx = jnp.where(live, code * per_slab + windows % per_slab, 0)
    live = live.astype(jnp.int32)

    swap = (here >= peers // 2).astype(jnp.int32).reshape(1)
    hop = [(s * groups + h, d * groups + (h ^ 1)) for s, d in middle for h in range(groups)]

    first = pack(swap, [keys, values], [(0, 0), (1, 0), (0, 1)], groups)
    crossed = send(first, across)
    rest = pack(swap, [keys, values], [(1, 1), (0, 2), (1, 2)], groups)
    rest = exchange(rest)
    most = pack(swap, [keys, values, query], [(2, 0), (2, 1), (2, 2), (0, 0), (1, 0), (0, 1)], groups)
    most = exchange(most)
    far_1 = send(after(rest[:, 0:1], crossed), across)
    far_2 = send(after(rest[:, 1:3], crossed), across)
    crossed = exchange(crossed)
    own = [most[:, 3:5], jnp.concatenate([most[:, 5:6], rest[:, 0:1]], axis=1), rest[:, 1:3]]
    before, behind = [None] * local, [None] * local
    for i in range(local):
        before[i] = send(own[i], right)
        behind[i] = send(own[i], left)
    second_2 = lax.ppermute(far_2, ("seq", "head"), hop)
    second_1 = send(far_1, middle)
    second_b = send(crossed, middle)
    parts = local

    def both(source, first=0):
        return ((source, first), (source, first + 1))

    takes = [
        ([most, before[0], behind[0], crossed, second_b], [both(0, 3), both(1), both(2), both(3), both(4)]),
        (
            [most, before[1], behind[1], rest, crossed, far_1, second_b, second_1],
            [((0, 5), (3, 0)), both(1), both(2), ((4, 2), (5, 0)), ((6, 2), (7, 0))],
        ),
        ([most, before[2], behind[2], rest, far_2, second_2], [both(3, 1), both(1), both(2), both(4), both(5)]),
    ]
    o = None
    for i, (sources, places) in enumerate(takes):
        o = attend(idx, live, sources, [[((0, i),)] + places], (i,), parts, o)
    o = exchange(o)
    return unpack(swap, o)


def solution(mesh):
    return jax.shard_map(
        body,
        mesh=mesh,
        in_specs=(
            P(("seq", "head"), None),
            P(("seq", "head"), None),
            P(("seq", "head"), None),
            P("seq", None),
        ),
        out_specs=P(("seq", "head"), None),
        check_vma=False,
    )
```

```python
import functools

import jax
import jax.numpy as jnp
from jax import lax
from jax.experimental import pallas as pl
from jax.experimental.pallas import tpu as pltpu
from jax.sharding import PartitionSpec as P


HD = 128
TFR = 4
PIECES = 1
SWAPPED = 2
SCALE2 = 1.4426950408889634 / HD**0.5


ANY = pl.BlockSpec(memory_space=pl.ANY)


def after(value, *first):
    return lax.optimization_barrier((value,) + first)[0]


def lane(g, head, local, swap):
    return pl.multiple_of(((g if swap is None else jnp.bitwise_xor(g, swap)) * local + head) * HD, HD)


def pack_kernel(picks, local, count, swap_ref, *refs):
    arrays, o_ref, sems = refs[:count], refs[count], refs[count + 1]
    copies = []
    for at, (array, head) in enumerate(picks):
        swap = swap_ref[0] if head == SWAPPED else None
        for g in range(o_ref.shape[0]):
            piece = arrays[array].at[:, pl.ds(lane(g, head, local, swap), HD)]
            copy = pltpu.make_async_copy(piece, o_ref.at[g, at], sems.at[at, g])
            copy.start()
            copies.append(copy)
    for copy in copies:
        copy.wait()


def pack(swap, arrays, picks, groups):
    rows, width = arrays[0].shape
    shape = (groups, len(picks), rows, HD)
    return pl.pallas_call(
        functools.partial(pack_kernel, picks, width // (groups * HD), len(arrays)),
        out_shape=jax.ShapeDtypeStruct(shape, arrays[0].dtype),
        grid_spec=pltpu.PrefetchScalarGridSpec(
            num_scalar_prefetch=1,
            grid=(1,),
            in_specs=[ANY] * len(arrays),
            out_specs=pl.BlockSpec(shape, lambda i, *_: (0, 0, 0, 0)),
            scratch_shapes=[pltpu.SemaphoreType.DMA((len(picks), groups))],
        ),
        cost_estimate=pl.CostEstimate(
            flops=0, bytes_accessed=4 * groups * len(picks) * rows * HD, transcendentals=0
        ),
        name="pack",
    )(swap, *arrays)


def unpack_kernel(swap_ref, part, o_ref, held, in_sems, sems):
    groups, local = part.shape[:2]
    arriving, leaving = [], []
    for g in range(groups):
        copy = pltpu.make_async_copy(part.at[g], held.at[g], in_sems.at[g])
        copy.start()
        arriving.append(copy)
    for g in range(groups):
        arriving[g].wait()
        for head in range(local):
            swap = swap_ref[0] if head == SWAPPED else None
            copy = pltpu.make_async_copy(
                held.at[g, head], o_ref.at[:, pl.ds(lane(g, head, local, swap), HD)], sems.at[head, g]
            )
            copy.start()
            leaving.append(copy)
    for copy in leaving:
        copy.wait()


def unpack(swap, part):
    groups, local, rows, _ = part.shape
    return pl.pallas_call(
        unpack_kernel,
        out_shape=jax.ShapeDtypeStruct((rows, groups * local * HD), part.dtype),
        grid_spec=pltpu.PrefetchScalarGridSpec(
            num_scalar_prefetch=1,
            grid=(1,),
            in_specs=[ANY],
            out_specs=ANY,
            scratch_shapes=[
                pltpu.VMEM(part.shape, part.dtype),
                pltpu.SemaphoreType.DMA((groups,)),
                pltpu.SemaphoreType.DMA((local, groups)),
            ],
        ),
        cost_estimate=pl.CostEstimate(
            flops=0, bytes_accessed=4 * groups * local * rows * HD, transcendentals=0
        ),
        name="unpack",
    )(swap, part)


def attend_kernel(tile, per_slab, plan, outs_at, count, idx_ref, live_ref, *refs):
    sources, refs = refs[:count], refs[count:]
    o_ref, held, q_held, o_held, s_held, sems, o_sems = refs[-7:]
    heads = len(plan)
    blocks, rows = sources[0].shape[0], sources[0].shape[2]
    slab = blocks * rows
    copies = []
    for h, taken in enumerate(plan):
        for at, parts in enumerate(taken):
            for n, (source, part) in enumerate(parts):
                into = q_held.at[h] if at == 0 else held.at[h, n, pl.ds((at - 1) * blocks, blocks)]
                copy = pltpu.make_async_copy(sources[source].at[:, part], into, sems.at[h, at, n])
                copy.start()
                copies.append((h, copy))
    flat = held.reshape(heads, 2, held.shape[2] * rows, HD)
    q_flat = q_held.reshape(heads, slab, HD)
    o_flat = o_held.reshape(heads, slab, HD)
    slots = idx_ref.shape[1]
    spans = tile // HD
    block = tile // PIECES

    begins = [[pl.multiple_of(idx_ref[t, j] * tile, 128) for j in range(slots)] for t in range(per_slab)]
    alive = [[live_ref[t, j] > 0 for j in range(slots)] for t in range(per_slab)]
    items = [(h, t, p) for h in range(heads) for t in range(per_slab) for p in range(PIECES)]

    def score(n, j, most):
        h, t, p = items[n]
        q = q_flat[h, pl.ds(t * tile + p * block, block), :]
        k = flat[h, 0, pl.ds(begins[t][j], tile), :]
        s = lax.dot_general(q, k, (((1,), (1,)), ((), ())), preferred_element_type=jnp.float32)
        s_held[n % 2, j] = s
        top = functools.reduce(jnp.maximum, [s[:, c * HD : (c + 1) * HD] for c in range(spans)])
        if j:
            top = jnp.where(alive[t][j], top, -jnp.inf)
        return top if most is None else jnp.maximum(most, top)

    def mix(n, j, top, total, mixed):
        h, t, _ = items[n]
        shift = jnp.where(alive[t][j], top, jnp.inf) if j else top
        expo = jnp.exp2(s_held[n % 2, j] * SCALE2 - shift)
        part = functools.reduce(jnp.add, [expo[:, c * HD : (c + 1) * HD] for c in range(spans)])
        v = flat[h, 1, pl.ds(begins[t][j], tile), :]
        pv = jnp.dot(expo.astype(jnp.bfloat16), v, preferred_element_type=jnp.float32)
        return (part, pv) if total is None else (total + part, mixed + pv)

    def arrive(head):
        for h, copy in copies:
            if h == head:
                copy.wait()

    arrive(0)
    most = None
    for j in range(slots):
        most = score(0, j, most)
    outs = []
    for n, (h, t, p) in enumerate(items):
        if n + 1 < len(items) and items[n + 1][0] != h:
            arrive(h + 1)
        top = jnp.max(most, axis=1, keepdims=True) * SCALE2
        most = total = mixed = None
        for j in range(slots):
            if n + 1 < len(items):
                most = score(n + 1, j, most)
            total, mixed = mix(n, j, top, total, mixed)
        total = jnp.sum(total, axis=1, keepdims=True)
        o_flat[h, pl.ds(t * tile + p * block, block), :] = (mixed / total).astype(o_flat.dtype)
        if t == per_slab - 1 and p == PIECES - 1:
            copy = pltpu.make_async_copy(o_held.at[h], o_ref.at[:, outs_at[h]], o_sems.at[h])
            copy.start()
            outs.append(copy)
    for copy in outs:
        copy.wait()


def attend(idx, live, sources, plan, outs_at, parts, into=None):
    per_slab, slots = idx.shape
    blocks, _, rows, _ = sources[0].shape
    slab = blocks * rows
    tile = slab // per_slab
    keys = slots * tile
    heads, columns = len(plan), len(plan[0]) - 1
    dtype = sources[0].dtype
    count = len(sources)
    held = [] if into is None else [into]
    return pl.pallas_call(
        functools.partial(attend_kernel, tile, per_slab, plan, outs_at, count),
        out_shape=jax.ShapeDtypeStruct((blocks, parts, rows, HD), dtype),
        grid_spec=pltpu.PrefetchScalarGridSpec(
            num_scalar_prefetch=2,
            grid=(1,),
            in_specs=[ANY] * (count + len(held)),
            out_specs=ANY,
            scratch_shapes=[
                pltpu.VMEM((heads, 2, columns * blocks, rows, HD), dtype),
                pltpu.VMEM((heads, blocks, rows, HD), dtype),
                pltpu.VMEM((heads, blocks, rows, HD), dtype),
                pltpu.VMEM((2, slots, tile // PIECES, tile), jnp.float32),
                pltpu.SemaphoreType.DMA((heads, columns + 1, 2)),
                pltpu.SemaphoreType.DMA((heads,)),
            ],
        ),
        input_output_aliases={2 + count: 0} if held else {},
        cost_estimate=pl.CostEstimate(
            flops=4 * heads * slab * keys * HD,
            bytes_accessed=4 * heads * slab * HD * (columns + 1),
            transcendentals=heads * slab * keys,
        ),
        name="attend",
    )(idx, live, *sources, *held)


def body(query, keys, values, windows):
    groups = lax.axis_size("head")
    peers = lax.axis_size("seq")
    columns = peers // TFR
    local = query.shape[1] // (groups * HD)
    per_slab = windows.shape[0]

    across = [(s, s ^ columns) for s in range(peers)]
    right = [(s, s + 1) for s in range(peers) if (s + 1) % columns]
    left = [(s, s - 1) for s in range(peers) if s % columns]
    middle = [(s, s + 2 * columns) for s in range(columns)] + [
        (s, s - 2 * columns) for s in range(3 * columns, peers)
    ]

    def send(x, pairs):
        return lax.ppermute(x, "seq", pairs)

    def exchange(x):
        return lax.all_to_all(x, "head", split_axis=0, concat_axis=0, tiled=True)

    here = lax.axis_index("seq")
    live = windows >= 0
    delta = windows // per_slab - here
    partner = jnp.where(here // columns % 2 == 0, columns, -columns)
    code = jnp.where(
        delta == 0,
        0,
        jnp.where(delta == -1, 1, jnp.where(delta == 1, 2, jnp.where(delta == partner, 3, 4))),
    )
    idx = jnp.where(live, code * per_slab + windows % per_slab, 0)
    live = live.astype(jnp.int32)

    swap = (here >= peers // 2).astype(jnp.int32).reshape(1)
    hop = [(s * groups + h, d * groups + (h ^ 1)) for s, d in middle for h in range(groups)]

    first = pack(swap, [keys, values], [(0, 0), (1, 0), (0, 1)], groups)
    crossed = send(first, across)
    rest = pack(swap, [keys, values], [(1, 1), (0, 2), (1, 2)], groups)
    rest = exchange(rest)
    most = pack(swap, [keys, values, query], [(2, 0), (2, 1), (2, 2), (0, 0), (1, 0), (0, 1)], groups)
    most = exchange(most)
    far_1 = send(after(rest[:, 0:1], crossed), across)
    far_2 = send(after(rest[:, 1:3], crossed), across)
    crossed = exchange(crossed)
    own = [most[:, 3:5], jnp.concatenate([most[:, 5:6], rest[:, 0:1]], axis=1), rest[:, 1:3]]
    before, behind = [None] * local, [None] * local
    for i in range(local):
        before[i] = send(own[i], right)
        behind[i] = send(own[i], left)
    second_2 = lax.ppermute(far_2, ("seq", "head"), hop)
    second_1 = send(far_1, middle)
    second_0 = send(crossed[:, 0:2], middle)
    second_k = send(crossed[:, 2:3], middle)
    parts = local

    def both(source, first=0):
        return ((source, first), (source, first + 1))

    takes = [
        ([most, before[0], behind[0], crossed, second_0], [both(0, 3), both(1), both(2), both(3), both(4)]),
        (
            [most, before[1], behind[1], rest, crossed, far_1, second_k, second_1],
            [((0, 5), (3, 0)), both(1), both(2), ((4, 2), (5, 0)), ((6, 0), (7, 0))],
        ),
        ([most, before[2], behind[2], rest, far_2, second_2], [both(3, 1), both(1), both(2), both(4), both(5)]),
    ]
    o = None
    for i, (sources, places) in enumerate(takes):
        o = attend(idx, live, sources, [[((0, i),)] + places], (i,), parts, o)
    o = exchange(o)
    return unpack(swap, o)


def solution(mesh):
    return jax.shard_map(
        body,
        mesh=mesh,
        in_specs=(
            P(("seq", "head"), None),
            P(("seq", "head"), None),
            P(("seq", "head"), None),
            P("seq", None),
        ),
        out_specs=P(("seq", "head"), None),
        check_vma=False,
    )
```

```python
import functools

import jax
import jax.numpy as jnp
from jax import lax
from jax.experimental import pallas as pl
from jax.experimental.pallas import tpu as pltpu
from jax.sharding import PartitionSpec as P


HD = 128
TFR = 4
PIECES = 1
SWAPPED = 2
SCALE2 = 1.4426950408889634 / HD**0.5


ANY = pl.BlockSpec(memory_space=pl.ANY)


def after(value, *first):
    return lax.optimization_barrier((value,) + first)[0]


def lane(g, head, local, swap):
    return pl.multiple_of(((g if swap is None else jnp.bitwise_xor(g, swap)) * local + head) * HD, HD)


def pack_kernel(picks, local, count, swap_ref, *refs):
    arrays, o_ref, sems = refs[:count], refs[count], refs[count + 1]
    copies = []
    for at, (array, head) in enumerate(picks):
        swap = swap_ref[0] if head == SWAPPED else None
        for g in range(o_ref.shape[0]):
            piece = arrays[array].at[:, pl.ds(lane(g, head, local, swap), HD)]
            copy = pltpu.make_async_copy(piece, o_ref.at[g, at], sems.at[at, g])
            copy.start()
            copies.append(copy)
    for copy in copies:
        copy.wait()


def pack(swap, arrays, picks, groups):
    rows, width = arrays[0].shape
    shape = (groups, len(picks), rows, HD)
    return pl.pallas_call(
        functools.partial(pack_kernel, picks, width // (groups * HD), len(arrays)),
        out_shape=jax.ShapeDtypeStruct(shape, arrays[0].dtype),
        grid_spec=pltpu.PrefetchScalarGridSpec(
            num_scalar_prefetch=1,
            grid=(1,),
            in_specs=[ANY] * len(arrays),
            out_specs=pl.BlockSpec(shape, lambda i, *_: (0, 0, 0, 0)),
            scratch_shapes=[pltpu.SemaphoreType.DMA((len(picks), groups))],
        ),
        cost_estimate=pl.CostEstimate(
            flops=0, bytes_accessed=4 * groups * len(picks) * rows * HD, transcendentals=0
        ),
        name="pack",
    )(swap, *arrays)


def unpack_kernel(swap_ref, part, o_ref, held, in_sems, sems):
    groups, local = part.shape[:2]
    arriving, leaving = [], []
    for g in range(groups):
        copy = pltpu.make_async_copy(part.at[g], held.at[g], in_sems.at[g])
        copy.start()
        arriving.append(copy)
    for g in range(groups):
        arriving[g].wait()
        for head in range(local):
            swap = swap_ref[0] if head == SWAPPED else None
            copy = pltpu.make_async_copy(
                held.at[g, head], o_ref.at[:, pl.ds(lane(g, head, local, swap), HD)], sems.at[head, g]
            )
            copy.start()
            leaving.append(copy)
    for copy in leaving:
        copy.wait()


def unpack(swap, part):
    groups, local, rows, _ = part.shape
    return pl.pallas_call(
        unpack_kernel,
        out_shape=jax.ShapeDtypeStruct((rows, groups * local * HD), part.dtype),
        grid_spec=pltpu.PrefetchScalarGridSpec(
            num_scalar_prefetch=1,
            grid=(1,),
            in_specs=[ANY],
            out_specs=ANY,
            scratch_shapes=[
                pltpu.VMEM(part.shape, part.dtype),
                pltpu.SemaphoreType.DMA((groups,)),
                pltpu.SemaphoreType.DMA((local, groups)),
            ],
        ),
        cost_estimate=pl.CostEstimate(
            flops=0, bytes_accessed=4 * groups * local * rows * HD, transcendentals=0
        ),
        name="unpack",
    )(swap, part)


def attend_kernel(tile, per_slab, plan, outs_at, count, idx_ref, live_ref, *refs):
    sources, refs = refs[:count], refs[count:]
    o_ref, held, q_held, o_held, s_held, sems, o_sems = refs[-7:]
    heads = len(plan)
    blocks, rows = sources[0].shape[0], sources[0].shape[2]
    slab = blocks * rows
    copies = []
    for h, taken in enumerate(plan):
        for n in range(2):
            for at, parts in enumerate(taken):
                if n == len(parts):
                    continue
                source, part = parts[n]
                into = q_held.at[h] if at == 0 else held.at[h, n, pl.ds((at - 1) * blocks, blocks)]
                copy = pltpu.make_async_copy(sources[source].at[:, part], into, sems.at[h, at, n])
                copy.start()
                copies.append(((h, n), copy))
    flat = held.reshape(heads, 2, held.shape[2] * rows, HD)
    q_flat = q_held.reshape(heads, slab, HD)
    o_flat = o_held.reshape(heads, slab, HD)
    slots = idx_ref.shape[1]
    spans = tile // HD
    block = tile // PIECES

    begins = [[pl.multiple_of(idx_ref[t, j] * tile, 128) for j in range(slots)] for t in range(per_slab)]
    alive = [[live_ref[t, j] > 0 for j in range(slots)] for t in range(per_slab)]
    items = [(h, t, p) for h in range(heads) for t in range(per_slab) for p in range(PIECES)]

    def score(n, j, most):
        h, t, p = items[n]
        q = q_flat[h, pl.ds(t * tile + p * block, block), :]
        k = flat[h, 0, pl.ds(begins[t][j], tile), :]
        s = lax.dot_general(q, k, (((1,), (1,)), ((), ())), preferred_element_type=jnp.float32)
        s_held[n % 2, j] = s
        top = functools.reduce(jnp.maximum, [s[:, c * HD : (c + 1) * HD] for c in range(spans)])
        if j:
            top = jnp.where(alive[t][j], top, -jnp.inf)
        return top if most is None else jnp.maximum(most, top)

    def mix(n, j, top, total, mixed):
        h, t, _ = items[n]
        shift = jnp.where(alive[t][j], top, jnp.inf) if j else top
        expo = jnp.exp2(s_held[n % 2, j] * SCALE2 - shift)
        part = functools.reduce(jnp.add, [expo[:, c * HD : (c + 1) * HD] for c in range(spans)])
        v = flat[h, 1, pl.ds(begins[t][j], tile), :]
        pv = jnp.dot(expo.astype(jnp.bfloat16), v, preferred_element_type=jnp.float32)
        return (part, pv) if total is None else (total + part, mixed + pv)

    def arrive(head, n):
        for which, copy in copies:
            if which == (head, n):
                copy.wait()

    arrive(0, 0)
    most = None
    for j in range(slots):
        most = score(0, j, most)
    outs = []
    for n, (h, t, p) in enumerate(items):
        if n + 1 < len(items) and items[n + 1][0] != h:
            arrive(h + 1, 0)
        if t == 0 and p == 0:
            arrive(h, 1)
        top = jnp.max(most, axis=1, keepdims=True) * SCALE2
        most = total = mixed = None
        for j in range(slots):
            if n + 1 < len(items):
                most = score(n + 1, j, most)
            total, mixed = mix(n, j, top, total, mixed)
        total = jnp.sum(total, axis=1, keepdims=True)
        o_flat[h, pl.ds(t * tile + p * block, block), :] = (mixed / total).astype(o_flat.dtype)
        if t == per_slab - 1 and p == PIECES - 1:
            copy = pltpu.make_async_copy(o_held.at[h], o_ref.at[:, outs_at[h]], o_sems.at[h])
            copy.start()
            outs.append(copy)
    for copy in outs:
        copy.wait()


def attend(idx, live, sources, plan, outs_at, parts, into=None):
    per_slab, slots = idx.shape
    blocks, _, rows, _ = sources[0].shape
    slab = blocks * rows
    tile = slab // per_slab
    keys = slots * tile
    heads, columns = len(plan), len(plan[0]) - 1
    dtype = sources[0].dtype
    count = len(sources)
    held = [] if into is None else [into]
    return pl.pallas_call(
        functools.partial(attend_kernel, tile, per_slab, plan, outs_at, count),
        out_shape=jax.ShapeDtypeStruct((blocks, parts, rows, HD), dtype),
        grid_spec=pltpu.PrefetchScalarGridSpec(
            num_scalar_prefetch=2,
            grid=(1,),
            in_specs=[ANY] * (count + len(held)),
            out_specs=ANY,
            scratch_shapes=[
                pltpu.VMEM((heads, 2, columns * blocks, rows, HD), dtype),
                pltpu.VMEM((heads, blocks, rows, HD), dtype),
                pltpu.VMEM((heads, blocks, rows, HD), dtype),
                pltpu.VMEM((2, slots, tile // PIECES, tile), jnp.float32),
                pltpu.SemaphoreType.DMA((heads, columns + 1, 2)),
                pltpu.SemaphoreType.DMA((heads,)),
            ],
        ),
        input_output_aliases={2 + count: 0} if held else {},
        cost_estimate=pl.CostEstimate(
            flops=4 * heads * slab * keys * HD,
            bytes_accessed=4 * heads * slab * HD * (columns + 1),
            transcendentals=heads * slab * keys,
        ),
        name="attend",
    )(idx, live, *sources, *held)


def body(query, keys, values, windows):
    groups = lax.axis_size("head")
    peers = lax.axis_size("seq")
    columns = peers // TFR
    local = query.shape[1] // (groups * HD)
    per_slab = windows.shape[0]

    across = [(s, s ^ columns) for s in range(peers)]
    right = [(s, s + 1) for s in range(peers) if (s + 1) % columns]
    left = [(s, s - 1) for s in range(peers) if s % columns]
    middle = [(s, s + 2 * columns) for s in range(columns)] + [
        (s, s - 2 * columns) for s in range(3 * columns, peers)
    ]

    def send(x, pairs):
        return lax.ppermute(x, "seq", pairs)

    def exchange(x):
        return lax.all_to_all(x, "head", split_axis=0, concat_axis=0, tiled=True)

    here = lax.axis_index("seq")
    live = windows >= 0
    delta = windows // per_slab - here
    partner = jnp.where(here // columns % 2 == 0, columns, -columns)
    code = jnp.where(
        delta == 0,
        0,
        jnp.where(delta == -1, 1, jnp.where(delta == 1, 2, jnp.where(delta == partner, 3, 4))),
    )
    idx = jnp.where(live, code * per_slab + windows % per_slab, 0)
    live = live.astype(jnp.int32)

    swap = (here >= peers // 2).astype(jnp.int32).reshape(1)
    hop = [(s * groups + h, d * groups + (h ^ 1)) for s, d in middle for h in range(groups)]

    first = pack(swap, [keys, values], [(0, 0), (1, 0), (0, 1)], groups)
    crossed = send(first, across)
    rest = pack(swap, [keys, values], [(1, 1), (0, 2), (1, 2)], groups)
    rest = exchange(rest)
    most = pack(swap, [keys, values, query], [(2, 0), (2, 1), (2, 2), (0, 0), (1, 0), (0, 1)], groups)
    most = exchange(most)
    far_1 = send(after(rest[:, 0:1], crossed), across)
    far_2 = send(after(rest[:, 1:3], crossed), across)
    crossed = exchange(crossed)
    before_a = send(rest, right)
    behind_a = send(rest, left)
    own = most[:, 3:6]
    before_b = send(own, right)
    behind_b = send(own, left)
    second_2 = lax.ppermute(far_2, ("seq", "head"), hop)
    second_1 = send(far_1, middle)
    second_b = send(crossed, middle)
    parts = local
    plan_0 = [[((0, 0),), ((0, 3), (0, 4)), ((1, 0), (1, 1)), ((2, 0), (2, 1)), ((3, 0), (3, 1)), ((4, 0), (4, 1))]]
    o = attend(idx, live, [most, before_b, behind_b, crossed, second_b], plan_0, (0,), parts)
    sources = [most, rest, before_a, behind_a, far_1, second_1, before_b, behind_b, crossed, second_b, second_2, far_2]
    plan = [
        [((0, 1),), ((0, 5), (1, 0)), ((6, 2), (2, 0)), ((7, 2), (3, 0)), ((8, 2), (4, 0)), ((9, 2), (5, 0))],
        [((0, 2),), ((1, 1), (1, 2)), ((2, 1), (2, 2)), ((3, 1), (3, 2)), ((11, 0), (11, 1)), ((10, 0), (10, 1))],
    ]
    o = attend(idx, live, sources, plan, (1, 2), parts, o)
    o = exchange(o)
    return unpack(swap, o)


def solution(mesh):
    return jax.shard_map(
        body,
        mesh=mesh,
        in_specs=(
            P(("seq", "head"), None),
            P(("seq", "head"), None),
            P(("seq", "head"), None),
            P("seq", None),
        ),
        out_specs=P(("seq", "head"), None),
        check_vma=False,
    )
```
